512 devices in a mesh: gx: 32 (over z, core), gy: 16 (over x, y).
Axes of the slice: x: 4, y: 4, z: 16, core: 2. Of those that a mesh axis runs over, the one named last changes fastest.
Arguments:
- snapshots: float32 [128, 256, 64, 128], P(None, 'gx', 'gy'), may hold values from -700 to 700
- viscosity: float32 [256, 64, 128], P('gx', 'gy'), may hold values from 0.2 to 1
- velocity: float32 [3, 256, 64, 128], P(None, 'gx', 'gy'), may hold values from -4 to 4
Outputs:
- modes: bfloat16 [128, 256, 64, 128], P(None, 'gx', 'gy')
- factor: float32 [128, 128], replicated
The draws below stay inside these ranges and needn't reach their ends.
All inputs are finite; a program needn't handle non-finite values.
Results may differ from the reference program's by a relative error of at most 0.001.
Values sent between devices are 32-bit elements; how exact they have to be, the bound alone decides.
No kernel may reach another device: no remote copies, remote signals or barrier semaphores. Data moves between devices by JAX's collectives and lax.ppermute only.
A program may use at most 64 MiB of HBM per device.

```python
import math
import jax
import jax.numpy as jnp
from jax import lax

SNAPS = 128
CZ = 128
NX = 256
NY = 64


def draw_snapshots(key, part):
    keys = jax.random.split(jax.random.fold_in(key, 7), 5)
    independent = jax.random.truncated_normal(keys[0], -4.0, 4.0, (SNAPS, NX, NY, CZ), jnp.float32)
    common = jax.random.truncated_normal(keys[1], -4.0, 4.0, (NX, NY, CZ), jnp.float32)
    mixing = jax.random.uniform(keys[2], (SNAPS,), jnp.float32, 0.3, 0.9)
    amplitude = jnp.exp(jax.random.uniform(keys[3], (SNAPS,), jnp.float32, 0.0, math.log(10.0)))
    rough = jnp.exp(jax.random.uniform(keys[4], (NX, NY, CZ), jnp.float32, math.log(0.5), math.log(2.0)))
    lagged = jnp.roll(independent, 1, axis=0)
    field = independent + 0.6 * lagged + mixing[:, None, None, None] * common[None]
    return (amplitude[:, None, None, None] * rough[None] * field).astype(jnp.float32)


def steps_of(rng, dims, cuts, low, top_value):
    level, own = 1.0, jax.random.fold_in(rng, 6)
    for dim, blocks in cuts:
        draws = jnp.exp(jax.random.uniform(jax.random.fold_in(own, dim), (blocks,), jnp.float32, low / len(cuts), top_value / len(cuts)))
        level = level * jnp.repeat(draws, dims[dim] // blocks).reshape([-1 if axis == dim else 1 for axis in range(len(dims))])
    return level


def scatter_about(key, extent, scale, limit, pieces=(), kind=jnp.bfloat16):
    values = jax.random.normal(key, extent, jnp.float32) * scale
    if len(pieces) > 0:
        values = steps_of(key, extent, pieces, -0.22, 0.18) * values
    return jnp.clip(values, min=-limit, max=limit).astype(kind)


def setup_inputs(seed: int = 0) -> dict:
    seeds = jax.random.split(jax.random.key(seed), 4)
    snapshots = draw_snapshots(jax.random.fold_in(seeds[3], 71), 0)
    viscosity = jnp.clip(0.2 + 0.8 * jax.random.uniform(seeds[1], (NX, NY, CZ), jnp.float32) ** steps_of(seeds[1], (NX, NY, CZ), ((0, 32), (1, 16)), -0.2, 0.2), 0.2, 1.0)
    velocity = scatter_about(seeds[2], (3, NX, NY, CZ), 1.0, 4.0, ((1, 32), (2, 16)), jnp.float32)
    return {"snapshots": snapshots, "viscosity": viscosity, "velocity": velocity}


def unit_shift(direction, offset):
    shifts = [0, 0, 0]
    shifts[direction] = offset
    return shifts

def take_cells(padded, shifts, sizes):
    return padded[..., 2 + shifts[0]:2 + shifts[0] + sizes[0], 2 + shifts[1]:2 + shifts[1] + sizes[1], 2 + shifts[2]:2 + shifts[2] + sizes[2]]

def stencil(field_pad, visc_pad, velocity):
    sizes = velocity.shape[1:]
    center = take_cells(field_pad, [0, 0, 0], sizes)
    visc_mid = take_cells(visc_pad, [0, 0, 0], sizes)
    total = jnp.zeros(center.shape, jnp.float32)
    for direction in range(3):
        plus_one = take_cells(field_pad, unit_shift(direction, 1), sizes)
        minus_one = take_cells(field_pad, unit_shift(direction, -1), sizes)
        plus_two = take_cells(field_pad, unit_shift(direction, 2), sizes)
        minus_two = take_cells(field_pad, unit_shift(direction, -2), sizes)
        slope = (8.0 * (plus_one - minus_one) - (plus_two - minus_two)) / 12.0
        visc_plus = 0.5 * (visc_mid + take_cells(visc_pad, unit_shift(direction, 1), sizes))
        visc_minus = 0.5 * (visc_mid + take_cells(visc_pad, unit_shift(direction, -1), sizes))
        spread = visc_plus * (plus_one - center) - visc_minus * (center - minus_one)
        total = total + velocity[direction] * slope - spread
    return total

def reference(snapshots, viscosity, velocity):
    visc_pad = jnp.pad(viscosity, 2)

    def one_snapshot(single):
        return stencil(jnp.pad(single, 2), visc_pad, velocity)
    resid = lax.map(one_snapshot, snapshots)
    count_cells = NX * NY * CZ
    matrix = resid.reshape(SNAPS, count_cells)
    gram = jnp.dot(matrix.astype(jnp.float32), matrix.T.astype(jnp.float32), precision=lax.Precision.HIGHEST, preferred_element_type=jnp.float32) / float(count_cells)
    factor = jnp.linalg.cholesky(gram).T
    solved = lax.linalg.triangular_solve(factor, matrix, left_side=True, lower=False, transpose_a=True)
    modes = solved.reshape(SNAPS, NX, NY, CZ).astype(jnp.bfloat16)
    return (modes, factor)
```

```python
import functools

import jax
import jax.numpy as jnp
from jax import lax
from jax.experimental import pallas as pl
from jax.experimental.pallas import tpu as pltpu
from jax.sharding import PartitionSpec as P

F32 = jnp.float32
BF16 = jnp.bfloat16
SN, NI, NJ, NZ = 128, 8, 4, 128
CELLS = NI * NJ
ROWS = SN * CELLS
GY_ROWS = 2 * NI * SN
GX_ROWS = 2 * NJ * SN
BLOCK = 8
VMEM = pl.BlockSpec(memory_space=pltpu.VMEM)
ANY = pl.BlockSpec(memory_space=pl.ANY)


def gy_at(j, i):
    return ((j % 2) * NI + i) * SN


def gx_at(layer, j):
    return (layer * NJ + j) * SN


def pack_kernel(u_hbm, visc, gyd, gyu, gxd, gxu, ubuf, sems):
    chunks = 4
    rows = ROWS // chunks
    copies = [
        pltpu.make_async_copy(
            u_hbm.at[pl.ds(k * rows, rows)], ubuf.at[pl.ds(k * rows, rows)], sems.at[k]
        )
        for k in range(chunks)
    ]
    for copy in copies:
        copy.start()
    for i in range(NI):
        for j in range(NJ):
            row = visc[pl.ds(i * NJ + j, 1), :]
            (gyd if j < 2 else gyu)[pl.ds(GY_ROWS + (j % 2) * NI + i, 1), :] = row
            if i < 2:
                gxd[pl.ds(GX_ROWS + i * NJ + j, 1), :] = row
            if i >= 6:
                gxu[pl.ds(GX_ROWS + (i - 6) * NJ + j, 1), :] = row
    groups = SN // 8 // chunks
    for k in range(chunks):
        copies[k].wait()

        def group(g, carry, k=k):
            first = pl.multiple_of((k * groups + g) * 8, 8)
            for i in range(NI):
                for j in range(NJ):
                    tile = ubuf[pl.ds(first * CELLS + i * NJ + j, 8, stride=CELLS), :]
                    (gyd if j < 2 else gyu)[pl.ds(gy_at(j, i) + first, 8), :] = tile
                    if i < 2:
                        gxd[pl.ds(gx_at(i, j) + first, 8), :] = tile
                    if i >= 6:
                        gxu[pl.ds(gx_at(i - 6, j) + first, 8), :] = tile
            return carry

        lax.fori_loop(0, groups, group, 0)


def local_kernel(gyd, gyu, hxm, hxp, visc, vel, out):
    lanes = lax.broadcasted_iota(jnp.int32, (8, NZ), 1)
    lane_row = lax.broadcasted_iota(jnp.int32, (1, NZ), 1)

    def source(i, j):
        if i < 0:
            return hxm, gx_at(i + 2, j)
        if i >= NI:
            return hxp, gx_at(i - NI, j)
        return (gyd if j < 2 else gyu), gy_at(j, i)

    def nu(i, j):
        if i < 0:
            return hxm[pl.ds(GX_ROWS + (i + 2) * NJ + j, 1), :]
        if i >= NI:
            return hxp[pl.ds(GX_ROWS + (i - NI) * NJ + j, 1), :]
        return visc[pl.ds(i * NJ + j, 1), :]

    def wide(row):
        return jnp.broadcast_to(row, (8, NZ))

    for i in range(NI):
        for j in range(NJ):
            mid = nu(i, j)
            vx, vy, vz = (vel[pl.ds(d * CELLS + i * NJ + j, 1), :] for d in range(3))
            ax8, ax1 = wide(vx * (8.0 / 12.0)), wide(vx * (1.0 / 12.0))
            az8, az1 = wide(vz * (8.0 / 12.0)), wide(vz * (1.0 / 12.0))
            ay8 = wide(vy * (8.0 / 12.0))
            xp, xm = wide(0.5 * (mid + nu(i + 1, j))), wide(0.5 * (mid + nu(i - 1, j)))
            nz_up = jnp.where(lane_row == NZ - 1, 0.0, pltpu.roll(mid, NZ - 1, 1))
            nz_dn = jnp.where(lane_row == 0, 0.0, pltpu.roll(mid, 1, 1))
            zp, zm = wide(0.5 * (mid + nz_up)), wide(0.5 * (mid + nz_dn))
            yp = wide(0.5 * (mid + nu(i, j + 1))) if j < NJ - 1 else None
            ym = wide(0.5 * (mid + nu(i, j - 1))) if j > 0 else None

            def group(g, carry, i=i, j=j):
                first = pl.multiple_of(g * 8, 8)

                def load(ii, jj):
                    ref, base = source(ii, jj)
                    return ref[pl.ds(base + first, 8), :]

                u = load(i, j)
                p1, m1, p2, m2 = load(i + 1, j), load(i - 1, j), load(i + 2, j), load(i - 2, j)
                total = ax8 * (p1 - m1) - ax1 * (p2 - m2)
                total = total - (xp * (p1 - u) - xm * (u - m1))
                p1 = jnp.where(lanes == NZ - 1, 0.0, pltpu.roll(u, NZ - 1, 1))
                p2 = jnp.where(lanes >= NZ - 2, 0.0, pltpu.roll(u, NZ - 2, 1))
                m1 = jnp.where(lanes == 0, 0.0, pltpu.roll(u, 1, 1))
                m2 = jnp.where(lanes < 2, 0.0, pltpu.roll(u, 2, 1))
                total = total + (az8 * (p1 - m1) - az1 * (p2 - m2))
                total = total - (zp * (p1 - u) - zm * (u - m1))
                if j < NJ - 1:
                    p1 = load(i, j + 1)
                    total = total - yp * (p1 - u)
                if j > 0:
                    m1 = load(i, j - 1)
                    total = total + ym * (u - m1)
                if 0 < j < NJ - 1:
                    total = total + ay8 * (p1 - m1)
                out[pl.ds((i * NJ + j) * SN + first, 8), :] = total
                return carry

            lax.fori_loop(0, SN // 8, group, 0, unroll=2)


def gram_kernel(scale, base, gyd, gyu, hym, hyp, visc, vel, split, gram, acc):
    acc[...] = jnp.zeros_like(acc)

    def wide(row):
        return jnp.broadcast_to(row, (16, NZ))

    for i in range(NI):
        mids = [visc[pl.ds(i * NJ + j, 1), :] for j in range(NJ)]
        vy = [vel[pl.ds(CELLS + i * NJ + j, 1), :] for j in range(NJ)]
        a8 = [wide(v * (8.0 / 12.0)) for v in vy]
        a1 = [wide(v * (1.0 / 12.0)) for v in vy]
        ym = wide(0.5 * (mids[0] + hym[pl.ds(GY_ROWS + NI + i, 1), :]))
        yp = wide(0.5 * (mids[3] + hyp[pl.ds(GY_ROWS + i, 1), :]))

        def group(g, carry, i=i, a8=a8, a1=a1, ym=ym, yp=yp):
            first = pl.multiple_of(g * 16, 16)

            def at(ref, j):
                return ref[pl.ds(gy_at(j, i) + first, 16), :]

            u0, u1, u2, u3 = at(gyd, 0), at(gyd, 1), at(gyu, 2), at(gyu, 3)
            m2, m1, p1, p2 = at(hym, 0), at(hym, 1), at(hyp, 0), at(hyp, 1)
            adds = [
                (a8[0] * (u1 - m1) - a1[0] * (u2 - m2)) + ym * (u0 - m1),
                -a1[1] * (u3 - m1),
                -a1[2] * (p1 - u0),
                (a8[3] * (p1 - u2) - a1[3] * (p2 - u1)) - yp * (p1 - u3),
            ]
            for j in range(NJ):
                cell = i * NJ + j
                value = base[pl.ds(cell * SN + first, 16), :] + adds[j]
                high = value.astype(BF16)
                low = (value - high.astype(F32)).astype(BF16)
                split[pl.ds(first, 16), cell * NZ : (cell + 1) * NZ] = high
                split[pl.ds(SN + first, 16), cell * NZ : (cell + 1) * NZ] = low
            return carry

        lax.fori_loop(0, SN // 16, group, 0)
        part = split[:, i * NJ * NZ : (i + 1) * NJ * NZ]
        acc[...] += lax.dot_general(
            part, part, (((1,), (1,)), ((), ())), preferred_element_type=F32
        )
    gram[...] = (
        (acc[:SN, :SN] + acc[SN:, SN:]) + (acc[:SN, SN:] + acc[SN:, :SN])
    ) * scale


def factorise(work, upper, inverse):
    lanes = lax.broadcasted_iota(jnp.int32, (8, SN), 1)
    width = BLOCK
    for base in range(0, SN, width):
        rows = [jnp.broadcast_to(work[base + k : base + k + 1, :], (8, SN)) for k in range(width)]
        entry = {}
        for r in range(width):
            for c in range(r + 1):
                entry[r, c] = jnp.broadcast_to(rows[c][:, base + r : base + r + 1], (8, SN))
        lower, inv, root = {}, {}, {}
        for k in range(width):
            inv[k] = 1.0 / entry[k, k]
            root[k] = lax.rsqrt(entry[k, k])
            for r in range(k + 1, width):
                lower[r, k] = entry[r, k] * inv[k]
                for c in range(k + 1, r + 1):
                    entry[r, c] = entry[r, c] - lower[r, k] * entry[c, k]
        inside = (lanes >= base) & (lanes < base + width)
        fwd, fwd_u, back = {}, {}, {}
        for k in range(width):
            z = jnp.where(inside, jnp.where(lanes == base + k, 1.0, 0.0), rows[k])
            zu = rows[k]
            for m in range(k):
                z = z - lower[k, m] * fwd[m]
                zu = zu - lower[k, m] * fwd_u[m]
            fwd[k], fwd_u[k] = z, zu
            upper[base + k : base + k + 1, :] = jnp.where(lanes >= base + k, zu * root[k], 0.0)[:1]
            inverse[base + k : base + k + 1, :] = jnp.where(lanes <= base + k, z * root[k], 0.0)[:1]
        for k in reversed(range(width)):
            y = fwd[k] * inv[k]
            for m in range(k + 1, width):
                y = y - lower[m, k] * back[m]
            back[k] = y
        for top in range(base + width, SN, 8):
            tile = work[top : top + 8, :]
            fresh = jnp.where(inside, 0.0, tile)
            for k in range(width):
                column = jnp.broadcast_to(tile[:, base + k : base + k + 1], (8, SN))
                fresh = fresh - column * back[k]
            work[top : top + 8, :] = fresh


def solve_kernel(gram, split, modes, upper, work, inverse, both, spread):
    work[...] = gram[...]
    factorise(work, upper, inverse)
    full = inverse[...]
    high = full.astype(BF16)
    low = (full - high.astype(F32)).astype(BF16)
    both[:SN, :SN] = high
    both[:SN, SN:] = high
    both[SN:, :SN] = low
    both[SN:, SN:] = low
    for cell in range(CELLS):
        product = jnp.dot(
            both[...], split[:, cell * NZ : (cell + 1) * NZ], preferred_element_type=F32
        )
        spread[pl.ds(cell, SN, stride=CELLS), :] = product[:SN] + product[SN:]

    def convert(g, carry):
        first = pl.multiple_of(g * 256, 256)
        modes[pl.ds(first, 256), :] = spread[pl.ds(first, 256), :].astype(BF16)
        return carry

    lax.fori_loop(0, ROWS // 256, convert, 0)


def shape(*dims, dtype=F32):
    return jax.ShapeDtypeStruct(dims, dtype)


def cost(flops, bytes_accessed):
    return pl.CostEstimate(flops=flops, bytes_accessed=bytes_accessed, transcendentals=0)


def whole_gram(gram):
    peers_y, peers_x = lax.axis_size("gy"), lax.axis_size("gx")
    rows = SN // peers_y
    parts = lax.all_to_all(gram.reshape(peers_y, rows, SN), "gy", 0, 0)
    mine = jnp.sum(parts, axis=0)
    parts = lax.all_to_all(jnp.broadcast_to(mine[None], (peers_x, rows, SN)), "gx", 0, 0)
    mine = jnp.sum(parts, axis=0)
    parts = lax.all_to_all(jnp.broadcast_to(mine[None], (peers_y, rows, SN)), "gy", 0, 0)
    return parts.reshape(SN, SN)


def per_device(snapshots, viscosity, velocity):
    flat = snapshots.reshape(ROWS, NZ)
    visc = viscosity.reshape(CELLS, NZ)
    vel = velocity.reshape(3 * CELLS, NZ)
    gyd, gyu, gxd, gxu = pl.pallas_call(
        pack_kernel,
        out_shape=(
            shape(GY_ROWS + 2 * NI, NZ),
            shape(GY_ROWS + 2 * NI, NZ),
            shape(GX_ROWS + 2 * NJ, NZ),
            shape(GX_ROWS + 2 * NJ, NZ),
        ),
        in_specs=[ANY, VMEM],
        out_specs=[VMEM] * 4,
        scratch_shapes=[pltpu.VMEM((ROWS, NZ), F32), pltpu.SemaphoreType.DMA((4,))],
        cost_estimate=cost(0, 6 << 20),
    )(flat, visc)

    def shifted(value, axis, step):
        peers = lax.axis_size(axis)
        pairs = [(k, k + step) for k in range(peers) if 0 <= k + step < peers]
        return lax.ppermute(value, axis, pairs)

    hym, hyp = shifted(gyu, "gy", 1), shifted(gyd, "gy", -1)
    hxm, hxp = shifted(gxu, "gx", 1), shifted(gxd, "gx", -1)
    base = pl.pallas_call(
        local_kernel,
        out_shape=shape(ROWS, NZ),
        in_specs=[VMEM] * 6,
        out_specs=VMEM,
        cost_estimate=cost(40 * ROWS * NZ, 5 << 20),
    )(gyd, gyu, hxm, hxp, visc, vel)
    count_cells = CELLS * NZ * lax.axis_size("gx") * lax.axis_size("gy")
    split, gram = pl.pallas_call(
        functools.partial(gram_kernel, 1.0 / count_cells),
        out_shape=(shape(2 * SN, CELLS * NZ, dtype=BF16), shape(SN, SN)),
        in_specs=[VMEM] * 7,
        out_specs=[VMEM] * 2,
        scratch_shapes=[pltpu.VMEM((2 * SN, 2 * SN), F32)],
        cost_estimate=cost(8 * SN * SN * CELLS * NZ, 8 << 20),
    )(base, gyd, gyu, hym, hyp, visc, vel)
    total = whole_gram(gram)
    modes, factor = pl.pallas_call(
        solve_kernel,
        out_shape=(shape(ROWS, NZ, dtype=BF16), shape(SN, SN)),
        in_specs=[VMEM] * 2,
        out_specs=[VMEM] * 2,
        scratch_shapes=[
            pltpu.VMEM((SN, SN), F32),
            pltpu.VMEM((SN, SN), F32),
            pltpu.VMEM((2 * SN, 2 * SN), BF16),
            pltpu.VMEM((ROWS, NZ), F32),
        ],
        cost_estimate=cost(8 * SN * SN * CELLS * NZ, 4 << 20),
    )(total, split)
    return modes.reshape(SN, NI, NJ, NZ), factor


def solution(mesh):
    placed = (P(None, "gx", "gy", None), P("gx", "gy", None), P(None, "gx", "gy", None))
    return jax.shard_map(
        per_device,
        mesh=mesh,
        in_specs=placed,
        out_specs=(P(None, "gx", "gy", None), P()),
        check_vma=False,
    )
```

```python
import functools

import jax
import jax.numpy as jnp
from jax import lax
from jax.experimental import pallas as pl
from jax.experimental.pallas import tpu as pltpu
from jax.sharding import PartitionSpec as P

F32 = jnp.float32
BF16 = jnp.bfloat16
SN, NI, NJ, NZ = 128, 8, 4, 128
CELLS = NI * NJ
ROWS = SN * CELLS
GY_ROWS = 2 * NI * SN
GX_ROWS = 2 * NJ * SN
BLOCK = 8
LIMIT = 20 << 20
VMEM = pl.BlockSpec(memory_space=pltpu.VMEM)
ANY = pl.BlockSpec(memory_space=pl.ANY)


def gy_at(j, i):
    return ((j % 2) * NI + i) * SN


def gx_at(layer, j):
    return (layer * NJ + j) * SN


def pack_kernel(u_hbm, visc_hbm, gyd, gyu, gxd, gxu, ubuf, visc, sems):
    chunks = 4
    small = pltpu.make_async_copy(visc_hbm, visc, sems.at[chunks])
    rows = ROWS // chunks
    copies = [
        pltpu.make_async_copy(
            u_hbm.at[pl.ds(k * rows, rows)], ubuf.at[pl.ds(k * rows, rows)], sems.at[k]
        )
        for k in range(chunks)
    ]
    for copy in copies:
        copy.start()
    small.start()
    groups = SN // 8 // chunks
    for k in range(chunks):
        copies[k].wait()

        def group(g, carry, k=k):
            first = pl.multiple_of((k * groups + g) * 8, 8)
            for i in range(NI):
                for j in range(NJ):
                    tile = ubuf[pl.ds(first * CELLS + i * NJ + j, 8, stride=CELLS), :]
                    (gyd if j < 2 else gyu)[pl.ds(gy_at(j, i) + first, 8), :] = tile
                    if i < 2:
                        gxd[pl.ds(gx_at(i, j) + first, 8), :] = tile
                    if i >= 6:
                        gxu[pl.ds(gx_at(i - 6, j) + first, 8), :] = tile
            return carry

        lax.fori_loop(0, groups, group, 0)
    small.wait()
    for i in range(NI):
        for j in range(NJ):
            row = visc[pl.ds(i * NJ + j, 1), :]
            (gyd if j < 2 else gyu)[pl.ds(GY_ROWS + (j % 2) * NI + i, 1), :] = row
            if i < 2:
                gxd[pl.ds(GX_ROWS + i * NJ + j, 1), :] = row
            if i >= 6:
                gxu[pl.ds(GX_ROWS + (i - 6) * NJ + j, 1), :] = row


def local_kernel(gyd, gyu, hxm, hxp, visc, vel, out):
    lanes = lax.broadcasted_iota(jnp.int32, (8, NZ), 1)
    lane_row = lax.broadcasted_iota(jnp.int32, (1, NZ), 1)

    def source(i, j):
        if i < 0:
            return hxm, gx_at(i + 2, j)
        if i >= NI:
            return hxp, gx_at(i - NI, j)
        return (gyd if j < 2 else gyu), gy_at(j, i)

    def nu(i, j):
        if i < 0:
            return hxm[pl.ds(GX_ROWS + (i + 2) * NJ + j, 1), :]
        if i >= NI:
            return hxp[pl.ds(GX_ROWS + (i - NI) * NJ + j, 1), :]
        return visc[pl.ds(i * NJ + j, 1), :]

    def wide(row):
        return jnp.broadcast_to(row, (8, NZ))

    for i in range(NI):
        for j in range(NJ):
            mid = nu(i, j)
            vx, vy, vz = (vel[pl.ds(d * CELLS + i * NJ + j, 1), :] for d in range(3))
            ax8, ax1 = wide(vx * (8.0 / 12.0)), wide(vx * (1.0 / 12.0))
            az8, az1 = wide(vz * (8.0 / 12.0)), wide(vz * (1.0 / 12.0))
            ay8 = wide(vy * (8.0 / 12.0))
            xp, xm = wide(0.5 * (mid + nu(i + 1, j))), wide(0.5 * (mid + nu(i - 1, j)))
            nz_up = jnp.where(lane_row == NZ - 1, 0.0, pltpu.roll(mid, NZ - 1, 1))
            nz_dn = jnp.where(lane_row == 0, 0.0, pltpu.roll(mid, 1, 1))
            zp, zm = wide(0.5 * (mid + nz_up)), wide(0.5 * (mid + nz_dn))
            yp = wide(0.5 * (mid + nu(i, j + 1))) if j < NJ - 1 else None
            ym = wide(0.5 * (mid + nu(i, j - 1))) if j > 0 else None

            def group(g, carry, i=i, j=j):
                first = g * 8

                def load(ii, jj):
                    ref, base = source(ii, jj)
                    return ref[pl.ds(base + first, 8), :]

                u = load(i, j)
                p1, m1, p2, m2 = load(i + 1, j), load(i - 1, j), load(i + 2, j), load(i - 2, j)
                total = ax8 * (p1 - m1) - ax1 * (p2 - m2)
                total = total - (xp * (p1 - u) - xm * (u - m1))
                p1 = jnp.where(lanes == NZ - 1, 0.0, pltpu.roll(u, NZ - 1, 1))
                p2 = jnp.where(lanes >= NZ - 2, 0.0, pltpu.roll(u, NZ - 2, 1))
                m1 = jnp.where(lanes == 0, 0.0, pltpu.roll(u, 1, 1))
                m2 = jnp.where(lanes < 2, 0.0, pltpu.roll(u, 2, 1))
                total = total + (az8 * (p1 - m1) - az1 * (p2 - m2))
                total = total - (zp * (p1 - u) - zm * (u - m1))
                if j < NJ - 1:
                    p1 = load(i, j + 1)
                    total = total - yp * (p1 - u)
                if j > 0:
                    m1 = load(i, j - 1)
                    total = total + ym * (u - m1)
                if 0 < j < NJ - 1:
                    total = total + ay8 * (p1 - m1)
                out[pl.ds((i * NJ + j) * SN + first, 8), :] = total
                return carry

            for g in range(SN // 8):
                group(g, 0)


def gram_kernel(scale, base, gyd, gyu, hym, hyp, visc, vel, split, gram, acc):
    acc[...] = jnp.zeros_like(acc)

    def wide(row):
        return jnp.broadcast_to(row, (16, NZ))

    for i in range(NI):
        mids = [visc[pl.ds(i * NJ + j, 1), :] for j in range(NJ)]
        vy = [vel[pl.ds(CELLS + i * NJ + j, 1), :] for j in range(NJ)]
        a8 = [wide(v * (8.0 / 12.0)) for v in vy]
        a1 = [wide(v * (1.0 / 12.0)) for v in vy]
        ym = wide(0.5 * (mids[0] + hym[pl.ds(GY_ROWS + NI + i, 1), :]))
        yp = wide(0.5 * (mids[3] + hyp[pl.ds(GY_ROWS + i, 1), :]))

        def group(g, carry, i=i, a8=a8, a1=a1, ym=ym, yp=yp):
            first = g * 16

            def at(ref, j):
                return ref[pl.ds(gy_at(j, i) + first, 16), :]

            u0, u1, u2, u3 = at(gyd, 0), at(gyd, 1), at(gyu, 2), at(gyu, 3)
            m2, m1, p1, p2 = at(hym, 0), at(hym, 1), at(hyp, 0), at(hyp, 1)
            adds = [
                (a8[0] * (u1 - m1) - a1[0] * (u2 - m2)) + ym * (u0 - m1),
                -a1[1] * (u3 - m1),
                -a1[2] * (p1 - u0),
                (a8[3] * (p1 - u2) - a1[3] * (p2 - u1)) - yp * (p1 - u3),
            ]
            for j in range(NJ):
                cell = i * NJ + j
                value = base[pl.ds(cell * SN + first, 16), :] + adds[j]
                high = value.astype(BF16)
                low = (value - high.astype(F32)).astype(BF16)
                split[pl.ds(first, 16), cell * NZ : (cell + 1) * NZ] = high
                split[pl.ds(SN + first, 16), cell * NZ : (cell + 1) * NZ] = low
            return carry

        for g in range(SN // 16):
            group(g, 0)
        part = split[:, i * NJ * NZ : (i + 1) * NJ * NZ]
        acc[...] += lax.dot_general(
            part, part, (((1,), (1,)), ((), ())), preferred_element_type=F32
        )
    gram[...] = (
        (acc[:SN, :SN] + acc[SN:, SN:]) + (acc[:SN, SN:] + acc[SN:, :SN])
    ) * scale


def factorise(work, upper, inverse):
    lanes = lax.broadcasted_iota(jnp.int32, (8, SN), 1)
    width = BLOCK
    for base in range(0, SN, width):
        rows = [jnp.broadcast_to(work[base + k : base + k + 1, :], (8, SN)) for k in range(width)]
        entry = {}
        for r in range(width):
            for c in range(r + 1):
                entry[r, c] = jnp.broadcast_to(rows[c][:, base + r : base + r + 1], (8, SN))
        lower, inv, root = {}, {}, {}
        for k in range(width):
            inv[k] = 1.0 / entry[k, k]
            root[k] = lax.rsqrt(entry[k, k])
            for r in range(k + 1, width):
                lower[r, k] = entry[r, k] * inv[k]
                for c in range(k + 1, r + 1):
                    entry[r, c] = entry[r, c] - lower[r, k] * entry[c, k]
        inside = (lanes >= base) & (lanes < base + width)
        fwd, fwd_u, back = {}, {}, {}
        for k in range(width):
            z = jnp.where(inside, jnp.where(lanes == base + k, 1.0, 0.0), rows[k])
            zu = rows[k]
            for m in range(k):
                z = z - lower[k, m] * fwd[m]
                zu = zu - lower[k, m] * fwd_u[m]
            fwd[k], fwd_u[k] = z, zu
            upper[base + k : base + k + 1, :] = jnp.where(lanes >= base + k, zu * root[k], 0.0)[:1]
            inverse[base + k : base + k + 1, :] = jnp.where(lanes <= base + k, z * root[k], 0.0)[:1]
        for k in reversed(range(width)):
            y = fwd[k] * inv[k]
            for m in range(k + 1, width):
                y = y - lower[m, k] * back[m]
            back[k] = y
        for top in range(base + width, SN, 8):
            tile = work[top : top + 8, :]
            fresh = jnp.where(inside, 0.0, tile)
            for k in range(width):
                column = jnp.broadcast_to(tile[:, base + k : base + k + 1], (8, SN))
                fresh = fresh - column * back[k]
            work[top : top + 8, :] = fresh


def solve_kernel(gram, split, modes, upper, work, inverse, both, spread):
    work[...] = gram[...]
    factorise(work, upper, inverse)
    full = inverse[...]
    high = full.astype(BF16)
    low = (full - high.astype(F32)).astype(BF16)
    both[:SN, :SN] = high
    both[:SN, SN:] = high
    both[SN:, :SN] = low
    both[SN:, SN:] = low
    for cell in range(CELLS):
        product = jnp.dot(
            both[...], split[:, cell * NZ : (cell + 1) * NZ], preferred_element_type=F32
        )
        spread[pl.ds(cell, SN, stride=CELLS), :] = product[:SN] + product[SN:]

    def convert(g, carry):
        first = pl.multiple_of(g * 256, 256)
        modes[pl.ds(first, 256), :] = spread[pl.ds(first, 256), :].astype(BF16)
        return carry

    lax.fori_loop(0, ROWS // 256, convert, 0)


def shape(*dims, dtype=F32):
    return jax.ShapeDtypeStruct(dims, dtype)


def onchip(*dims, dtype=F32):
    return pltpu.VMEM(dims, dtype)


def far(*values):
    return [pltpu.with_memory_space_constraint(v, pltpu.HBM) for v in values]


def near(*values):
    return [pltpu.with_memory_space_constraint(v, pltpu.VMEM) for v in values]


def cost(flops, bytes_accessed):
    return pl.CostEstimate(flops=flops, bytes_accessed=bytes_accessed, transcendentals=0)


def whole_gram(gram):
    peers_y, peers_x = lax.axis_size("gy"), lax.axis_size("gx")
    rows = SN // peers_y
    parts = lax.all_to_all(gram.reshape(peers_y, rows, SN), "gy", 0, 0)
    mine = jnp.sum(parts, axis=0)
    parts = lax.all_to_all(jnp.broadcast_to(mine[None], (peers_x, rows, SN)), "gx", 0, 0)
    mine = jnp.sum(parts, axis=0)
    parts = lax.all_to_all(jnp.broadcast_to(mine[None], (peers_y, rows, SN)), "gy", 0, 0)
    return parts.reshape(SN, SN)


def per_device(snapshots, viscosity, velocity):
    flat = snapshots.reshape(ROWS, NZ)
    visc = viscosity.reshape(CELLS, NZ)
    vel = velocity.reshape(3 * CELLS, NZ)
    gyd, gyu, gxd, gxu = pl.pallas_call(
        pack_kernel,
        out_shape=(
            onchip(GY_ROWS + 2 * NI, NZ),
            onchip(GY_ROWS + 2 * NI, NZ),
            onchip(GX_ROWS + 2 * NJ, NZ),
            onchip(GX_ROWS + 2 * NJ, NZ),
        ),
        in_specs=[ANY, ANY],
        out_specs=[VMEM] * 4,
        scratch_shapes=[
            pltpu.VMEM((ROWS, NZ), F32),
            pltpu.VMEM((CELLS, NZ), F32),
            pltpu.SemaphoreType.DMA((5,)),
        ],
        compiler_params=pltpu.CompilerParams(vmem_limit_bytes=LIMIT),
        cost_estimate=cost(0, 6 << 20),
    )(*far(flat, visc))

    def shifted(value, axis, step):
        peers = lax.axis_size(axis)
        pairs = [(k, k + step) for k in range(peers) if 0 <= k + step < peers]
        return lax.ppermute(value, axis, pairs)

    hym, hyp = shifted(gyu, "gy", 1), shifted(gyd, "gy", -1)
    hxm, hxp = shifted(gxu, "gx", 1), shifted(gxd, "gx", -1)
    base = pl.pallas_call(
        local_kernel,
        out_shape=onchip(ROWS, NZ),
        in_specs=[VMEM] * 6,
        out_specs=VMEM,
        compiler_params=pltpu.CompilerParams(vmem_limit_bytes=LIMIT),
        cost_estimate=cost(40 * ROWS * NZ, 5 << 20),
    )(*near(gyd, gyu, hxm, hxp), visc, vel)
    count_cells = CELLS * NZ * lax.axis_size("gx") * lax.axis_size("gy")
    split, gram = pl.pallas_call(
        functools.partial(gram_kernel, 1.0 / count_cells),
        out_shape=(onchip(2 * SN, CELLS * NZ, dtype=BF16), onchip(SN, SN)),
        in_specs=[VMEM] * 7,
        out_specs=[VMEM] * 2,
        scratch_shapes=[pltpu.VMEM((2 * SN, 2 * SN), F32)],
        compiler_params=pltpu.CompilerParams(vmem_limit_bytes=LIMIT),
        cost_estimate=cost(8 * SN * SN * CELLS * NZ, 8 << 20),
    )(*near(base, gyd, gyu, hym, hyp), visc, vel)
    total = whole_gram(gram)
    modes, factor = pl.pallas_call(
        solve_kernel,
        out_shape=(shape(ROWS, NZ, dtype=BF16), shape(SN, SN)),
        in_specs=[VMEM] * 2,
        out_specs=[VMEM] * 2,
        scratch_shapes=[
            pltpu.VMEM((SN, SN), F32),
            pltpu.VMEM((SN, SN), F32),
            pltpu.VMEM((2 * SN, 2 * SN), BF16),
            pltpu.VMEM((ROWS, NZ), F32),
        ],
        compiler_params=pltpu.CompilerParams(vmem_limit_bytes=LIMIT),
        cost_estimate=cost(8 * SN * SN * CELLS * NZ, 4 << 20),
    )(*near(total, split))
    return modes.reshape(SN, NI, NJ, NZ), factor


def solution(mesh):
    placed = (P(None, "gx", "gy", None), P("gx", "gy", None), P(None, "gx", "gy", None))
    return jax.shard_map(
        per_device,
        mesh=mesh,
        in_specs=placed,
        out_specs=(P(None, "gx", "gy", None), P()),
        check_vma=False,
    )
```

```python
import functools

import jax
import jax.numpy as jnp
from jax import lax
from jax.experimental import pallas as pl
from jax.experimental.pallas import tpu as pltpu
from jax.sharding import PartitionSpec as P

F32 = jnp.float32
BF16 = jnp.bfloat16
SN, NI, NJ, NZ = 128, 8, 4, 128
CELLS = NI * NJ
ROWS = SN * CELLS
GY_ROWS = 2 * NI * SN
GX_ROWS = 2 * NJ * SN
BLOCK = 8
PITCH = CELLS + 1
LIMIT = 20 << 20
VMEM = pl.BlockSpec(memory_space=pltpu.VMEM)
ANY = pl.BlockSpec(memory_space=pl.ANY)


def gy_at(j, i):
    return ((j % 2) * NI + i) * SN


def gx_at(layer, j):
    return (layer * NJ + j) * SN


def pack_kernel(u_hbm, visc_hbm, gyd, gyu, gxd, gxu, ubuf, turned, visc, sems):
    chunks = 4
    small = pltpu.make_async_copy(visc_hbm, visc, sems.at[chunks])
    rows = ROWS // chunks
    copies = [
        pltpu.make_async_copy(
            u_hbm.at[pl.ds(k * rows, rows)], ubuf.at[pl.ds(k * rows, rows)], sems.at[k]
        )
        for k in range(chunks)
    ]
    for copy in copies:
        copy.start()
    small.start()
    for k in range(chunks):
        copies[k].wait()
        for snap in range(k * SN // chunks, (k + 1) * SN // chunks):
            for part in range(0, CELLS, 8):
                turned[snap * PITCH + part : snap * PITCH + part + 8, :] = ubuf[
                    snap * CELLS + part : snap * CELLS + part + 8, :
                ]
        for first in range(k * SN // chunks, (k + 1) * SN // chunks, 8):
            for i in range(NI):
                for j in range(NJ):
                    tile = turned[pl.ds(first * PITCH + i * NJ + j, 8, stride=PITCH), :]
                    (gyd if j < 2 else gyu)[pl.ds(gy_at(j, i) + first, 8), :] = tile
                    if i < 2:
                        gxd[pl.ds(gx_at(i, j) + first, 8), :] = tile
                    if i >= 6:
                        gxu[pl.ds(gx_at(i - 6, j) + first, 8), :] = tile
    small.wait()
    for i in range(NI):
        for j in range(NJ):
            row = visc[pl.ds(i * NJ + j, 1), :]
            (gyd if j < 2 else gyu)[pl.ds(GY_ROWS + (j % 2) * NI + i, 1), :] = row
            if i < 2:
                gxd[pl.ds(GX_ROWS + i * NJ + j, 1), :] = row
            if i >= 6:
                gxu[pl.ds(GX_ROWS + (i - 6) * NJ + j, 1), :] = row


def local_kernel(gyd, gyu, hxm, hxp, visc, vel, out):
    lanes = lax.broadcasted_iota(jnp.int32, (8, NZ), 1)
    lane_row = lax.broadcasted_iota(jnp.int32, (1, NZ), 1)

    def source(i, j):
        if i < 0:
            return hxm, gx_at(i + 2, j)
        if i >= NI:
            return hxp, gx_at(i - NI, j)
        return (gyd if j < 2 else gyu), gy_at(j, i)

    def nu(i, j):
        if i < 0:
            return hxm[pl.ds(GX_ROWS + (i + 2) * NJ + j, 1), :]
        if i >= NI:
            return hxp[pl.ds(GX_ROWS + (i - NI) * NJ + j, 1), :]
        return visc[pl.ds(i * NJ + j, 1), :]

    def wide(row):
        return jnp.broadcast_to(row, (8, NZ))

    for i in range(NI):
        for j in range(NJ):
            mid = nu(i, j)
            vx, vy, vz = (vel[pl.ds(d * CELLS + i * NJ + j, 1), :] for d in range(3))
            ax8, ax1 = wide(vx * (8.0 / 12.0)), wide(vx * (1.0 / 12.0))
            az8, az1 = wide(vz * (8.0 / 12.0)), wide(vz * (1.0 / 12.0))
            ay8 = wide(vy * (8.0 / 12.0))
            xp, xm = wide(0.5 * (mid + nu(i + 1, j))), wide(0.5 * (mid + nu(i - 1, j)))
            nz_up = jnp.where(lane_row == NZ - 1, 0.0, pltpu.roll(mid, NZ - 1, 1))
            nz_dn = jnp.where(lane_row == 0, 0.0, pltpu.roll(mid, 1, 1))
            zp, zm = wide(0.5 * (mid + nz_up)), wide(0.5 * (mid + nz_dn))
            yp = wide(0.5 * (mid + nu(i, j + 1))) if j < NJ - 1 else None
            ym = wide(0.5 * (mid + nu(i, j - 1))) if j > 0 else None

            def group(g, carry, i=i, j=j):
                first = g * 8

                def load(ii, jj):
                    ref, base = source(ii, jj)
                    return ref[pl.ds(base + first, 8), :]

                u = load(i, j)
                p1, m1, p2, m2 = load(i + 1, j), load(i - 1, j), load(i + 2, j), load(i - 2, j)
                total = ax8 * (p1 - m1) - ax1 * (p2 - m2)
                total = total - (xp * (p1 - u) - xm * (u - m1))
                p1 = jnp.where(lanes == NZ - 1, 0.0, pltpu.roll(u, NZ - 1, 1))
                p2 = jnp.where(lanes >= NZ - 2, 0.0, pltpu.roll(u, NZ - 2, 1))
                m1 = jnp.where(lanes == 0, 0.0, pltpu.roll(u, 1, 1))
                m2 = jnp.where(lanes < 2, 0.0, pltpu.roll(u, 2, 1))
                total = total + (az8 * (p1 - m1) - az1 * (p2 - m2))
                total = total - (zp * (p1 - u) - zm * (u - m1))
                if j < NJ - 1:
                    p1 = load(i, j + 1)
                    total = total - yp * (p1 - u)
                if j > 0:
                    m1 = load(i, j - 1)
                    total = total + ym * (u - m1)
                if 0 < j < NJ - 1:
                    total = total + ay8 * (p1 - m1)
                out[pl.ds((i * NJ + j) * SN + first, 8), :] = total
                return carry

            for g in range(SN // 8):
                group(g, 0)


def gram_kernel(scale, base, gyd, gyu, hym, hyp, visc, vel, split, gram, acc):
    acc[...] = jnp.zeros_like(acc)

    def wide(row):
        return jnp.broadcast_to(row, (16, NZ))

    for i in range(NI):
        mids = [visc[pl.ds(i * NJ + j, 1), :] for j in range(NJ)]
        vy = [vel[pl.ds(CELLS + i * NJ + j, 1), :] for j in range(NJ)]
        a8 = [wide(v * (8.0 / 12.0)) for v in vy]
        a1 = [wide(v * (1.0 / 12.0)) for v in vy]
        ym = wide(0.5 * (mids[0] + hym[pl.ds(GY_ROWS + NI + i, 1), :]))
        yp = wide(0.5 * (mids[3] + hyp[pl.ds(GY_ROWS + i, 1), :]))

        def group(g, carry, i=i, a8=a8, a1=a1, ym=ym, yp=yp):
            first = g * 16

            def at(ref, j):
                return ref[pl.ds(gy_at(j, i) + first, 16), :]

            u0, u1, u2, u3 = at(gyd, 0), at(gyd, 1), at(gyu, 2), at(gyu, 3)
            m2, m1, p1, p2 = at(hym, 0), at(hym, 1), at(hyp, 0), at(hyp, 1)
            adds = [
                (a8[0] * (u1 - m1) - a1[0] * (u2 - m2)) + ym * (u0 - m1),
                -a1[1] * (u3 - m1),
                -a1[2] * (p1 - u0),
                (a8[3] * (p1 - u2) - a1[3] * (p2 - u1)) - yp * (p1 - u3),
            ]
            for j in range(NJ):
                cell = i * NJ + j
                value = base[pl.ds(cell * SN + first, 16), :] + adds[j]
                high = value.astype(BF16)
                low = (value - high.astype(F32)).astype(BF16)
                split[pl.ds(first, 16), cell * NZ : (cell + 1) * NZ] = high
                split[pl.ds(SN + first, 16), cell * NZ : (cell + 1) * NZ] = low
            return carry

        for g in range(SN // 16):
            group(g, 0)
        part = split[:, i * NJ * NZ : (i + 1) * NJ * NZ]
        acc[...] += lax.dot_general(
            part, part, (((1,), (1,)), ((), ())), preferred_element_type=F32
        )
    gram[...] = (
        (acc[:SN, :SN] + acc[SN:, SN:]) + (acc[:SN, SN:] + acc[SN:, :SN])
    ) * scale


def spread_lane(row, lane):
    return jnp.take_along_axis(row, jnp.full((8, SN), lane, jnp.int32), axis=1)


def factorise(work, upper, inverse):
    lanes = lax.broadcasted_iota(jnp.int32, (8, SN), 1)
    width = BLOCK
    for base in range(0, SN, width):
        rows = [jnp.broadcast_to(work[base + k : base + k + 1, :], (8, SN)) for k in range(width)]
        entry = {}
        for r in range(width):
            for c in range(r + 1):
                entry[r, c] = spread_lane(rows[c], base + r)
        lower, inv, root = {}, {}, {}
        for k in range(width):
            inv[k] = 1.0 / entry[k, k]
            root[k] = lax.rsqrt(entry[k, k])
            for r in range(k + 1, width):
                lower[r, k] = entry[r, k] * inv[k]
                for c in range(k + 1, r + 1):
                    entry[r, c] = entry[r, c] - lower[r, k] * entry[c, k]
        inside = (lanes >= base) & (lanes < base + width)
        fwd, fwd_u, back = {}, {}, {}
        for k in range(width):
            z = jnp.where(inside, jnp.where(lanes == base + k, 1.0, 0.0), rows[k])
            zu = rows[k]
            for m in range(k):
                z = z - lower[k, m] * fwd[m]
                zu = zu - lower[k, m] * fwd_u[m]
            fwd[k], fwd_u[k] = z, zu
            upper[base + k : base + k + 1, :] = jnp.where(lanes >= base + k, zu * root[k], 0.0)[:1]
            inverse[base + k : base + k + 1, :] = jnp.where(lanes <= base + k, z * root[k], 0.0)[:1]
        first = base + width
        if first < SN:
            tile = work[first : first + 8, :]
            fresh = jnp.where(inside, 0.0, tile)
            columns = {}
            for k in range(width):
                column = jnp.broadcast_to(tile[:, base + k : base + k + 1], (8, SN))
                for m in range(k):
                    column = column - lower[k, m] * columns[m]
                columns[k] = column
                fresh = fresh - column * (fwd[k] * inv[k])
            work[first : first + 8, :] = fresh
        for k in reversed(range(width)):
            y = fwd[k] * inv[k]
            for m in range(k + 1, width):
                y = y - lower[m, k] * back[m]
            back[k] = y
        for top in range(first + 8, SN, 8):
            tile = work[top : top + 8, :]
            fresh = jnp.where(inside, 0.0, tile)
            for k in range(width):
                column = jnp.broadcast_to(tile[:, base + k : base + k + 1], (8, SN))
                fresh = fresh - column * back[k]
            work[top : top + 8, :] = fresh


def solve_kernel(gram, split, modes, upper, work, inverse, both, spread):
    work[...] = gram[...]
    factorise(work, upper, inverse)
    full = inverse[...]
    high = full.astype(BF16)
    low = (full - high.astype(F32)).astype(BF16)
    both[:SN, :SN] = high
    both[:SN, SN:] = high
    both[SN:, :SN] = low
    both[SN:, SN:] = low
    for cell in range(0, CELLS, 2):
        product = jnp.dot(
            both[...], split[:, cell * NZ : (cell + 2) * NZ], preferred_element_type=F32
        )
        total = product[:SN] + product[SN:]
        spread[pl.ds(cell, SN, stride=PITCH), :] = total[:, :NZ]
        spread[pl.ds(cell + 1, SN, stride=PITCH), :] = total[:, NZ:]
    for snap in range(SN):
        modes[snap * CELLS : (snap + 1) * CELLS, :] = spread[
            snap * PITCH : snap * PITCH + CELLS, :
        ].astype(BF16)


def shape(*dims, dtype=F32):
    return jax.ShapeDtypeStruct(dims, dtype)


def onchip(*dims, dtype=F32):
    return pltpu.VMEM(dims, dtype)


def far(*values):
    return [pltpu.with_memory_space_constraint(v, pltpu.HBM) for v in values]


def near(*values):
    return [pltpu.with_memory_space_constraint(v, pltpu.VMEM) for v in values]


def cost(flops, bytes_accessed):
    return pl.CostEstimate(flops=flops, bytes_accessed=bytes_accessed, transcendentals=0)


def whole_gram(gram):
    peers_y, peers_x = lax.axis_size("gy"), lax.axis_size("gx")
    rows = SN // peers_y
    parts = lax.all_to_all(gram.reshape(peers_y, rows, SN), "gy", 0, 0)
    mine = jnp.sum(parts, axis=0)
    parts = lax.all_to_all(jnp.broadcast_to(mine[None], (peers_x, rows, SN)), "gx", 0, 0)
    mine = jnp.sum(parts, axis=0)
    parts = lax.all_to_all(jnp.broadcast_to(mine[None], (peers_y, rows, SN)), "gy", 0, 0)
    return parts.reshape(SN, SN)


def per_device(snapshots, viscosity, velocity):
    flat = snapshots.reshape(ROWS, NZ)
    visc = viscosity.reshape(CELLS, NZ)
    vel = velocity.reshape(3 * CELLS, NZ)
    gyd, gyu, gxd, gxu = pl.pallas_call(
        pack_kernel,
        out_shape=(
            onchip(GY_ROWS + 2 * NI, NZ),
            onchip(GY_ROWS + 2 * NI, NZ),
            onchip(GX_ROWS + 2 * NJ, NZ),
            onchip(GX_ROWS + 2 * NJ, NZ),
        ),
        in_specs=[ANY, ANY],
        out_specs=[VMEM] * 4,
        scratch_shapes=[
            pltpu.VMEM((ROWS, NZ), F32),
            pltpu.VMEM((SN * PITCH, NZ), F32),
            pltpu.VMEM((CELLS, NZ), F32),
            pltpu.SemaphoreType.DMA((5,)),
        ],
        compiler_params=pltpu.CompilerParams(vmem_limit_bytes=LIMIT),
        cost_estimate=cost(0, 6 << 20),
    )(*far(flat, visc))

    def shifted(value, axis, step):
        peers = lax.axis_size(axis)
        pairs = [(k, k + step) for k in range(peers) if 0 <= k + step < peers]
        return lax.ppermute(value, axis, pairs)

    hym, hyp = shifted(gyu, "gy", 1), shifted(gyd, "gy", -1)
    hxm, hxp = shifted(gxu, "gx", 1), shifted(gxd, "gx", -1)
    base = pl.pallas_call(
        local_kernel,
        out_shape=onchip(ROWS, NZ),
        in_specs=[VMEM] * 6,
        out_specs=VMEM,
        compiler_params=pltpu.CompilerParams(vmem_limit_bytes=LIMIT),
        cost_estimate=cost(40 * ROWS * NZ, 5 << 20),
    )(*near(gyd, gyu, hxm, hxp), visc, vel)
    count_cells = CELLS * NZ * lax.axis_size("gx") * lax.axis_size("gy")
    split, gram = pl.pallas_call(
        functools.partial(gram_kernel, 1.0 / count_cells),
        out_shape=(onchip(2 * SN, CELLS * NZ, dtype=BF16), onchip(SN, SN)),
        in_specs=[VMEM] * 7,
        out_specs=[VMEM] * 2,
        scratch_shapes=[pltpu.VMEM((2 * SN, 2 * SN), F32)],
        compiler_params=pltpu.CompilerParams(vmem_limit_bytes=LIMIT),
        cost_estimate=cost(8 * SN * SN * CELLS * NZ, 8 << 20),
    )(*near(base, gyd, gyu, hym, hyp), visc, vel)
    total = whole_gram(gram)
    modes, factor = pl.pallas_call(
        solve_kernel,
        out_shape=(shape(ROWS, NZ, dtype=BF16), shape(SN, SN)),
        in_specs=[VMEM] * 2,
        out_specs=[VMEM] * 2,
        scratch_shapes=[
            pltpu.VMEM((SN, SN), F32),
            pltpu.VMEM((SN, SN), F32),
            pltpu.VMEM((2 * SN, 2 * SN), BF16),
            pltpu.VMEM((SN * PITCH, NZ), F32),
        ],
        compiler_params=pltpu.CompilerParams(vmem_limit_bytes=LIMIT),
        cost_estimate=cost(8 * SN * SN * CELLS * NZ, 4 << 20),
    )(*near(total, split))
    return modes.reshape(SN, NI, NJ, NZ), factor


def solution(mesh):
    placed = (P(None, "gx", "gy", None), P("gx", "gy", None), P(None, "gx", "gy", None))
    return jax.shard_map(
        per_device,
        mesh=mesh,
        in_specs=placed,
        out_specs=(P(None, "gx", "gy", None), P()),
        check_vma=False,
    )
```

```python
import functools

import jax
import jax.numpy as jnp
from jax import lax
from jax.experimental import pallas as pl
from jax.experimental.pallas import tpu as pltpu
from jax.sharding import PartitionSpec as P


F32 = jnp.float32
BF16 = jnp.bfloat16
SN, NI, NJ, NZ = 128, 8, 4, 128
HALF = SN // 2
CELLS = NI * NJ
ROWS = SN * CELLS
GY_ROWS = 2 * NI * HALF
GX_ROWS = 2 * NJ * SN
BLOCK = 8
PITCH = CELLS + 1
LIMIT = 20 << 20
VMEM = pl.BlockSpec(memory_space=pltpu.VMEM)
ANY = pl.BlockSpec(memory_space=pl.ANY)


def gy_at(j, i):
    return ((j % 2) * NI + i) * HALF


def gx_at(layer, j):
    return (layer * NJ + j) * SN


def fetches(u_hbm, ubuf, sems, half, chunks):
    rows = ROWS // 2 // chunks
    return [
        pltpu.make_async_copy(
            u_hbm.at[pl.ds(half * (ROWS // 2) + k * rows, rows)],
            ubuf.at[pl.ds(k * rows, rows)],
            sems.at[k],
        )
        for k in range(chunks)
    ]


def turn(ubuf, turned, start, stop):
    for snap in range(start, stop):
        for part in range(0, CELLS, 8):
            turned[snap * PITCH + part : snap * PITCH + part + 8, :] = ubuf[
                snap * CELLS + part : snap * CELLS + part + 8, :
            ]


def first_pack_kernel(u_hbm, visc_hbm, gyd, gyu, ubuf, turned, visc, sems):
    chunks = 2
    small = pltpu.make_async_copy(visc_hbm, visc, sems.at[chunks])
    copies = fetches(u_hbm, ubuf, sems, 0, chunks)
    for copy in copies:
        copy.start()
    small.start()
    for k in range(chunks):
        copies[k].wait()
        start, stop = k * HALF // chunks, (k + 1) * HALF // chunks
        turn(ubuf, turned, start, stop)
        for first in range(start, stop, 8):
            for i in range(NI):
                for j in range(NJ):
                    tile = turned[pl.ds(first * PITCH + i * NJ + j, 8, stride=PITCH), :]
                    (gyd if j < 2 else gyu)[pl.ds(gy_at(j, i) + first, 8), :] = tile
    small.wait()
    for i in range(NI):
        for j in range(NJ):
            row = visc[pl.ds(i * NJ + j, 1), :]
            (gyd if j < 2 else gyu)[pl.ds(GY_ROWS + (j % 2) * NI + i, 1), :] = row


def second_pack_kernel(u_hbm, gyd_a, gyu_a, gyd, gyu, gxd, gxu, ubuf, turned, sems):
    chunks = 2
    copies = fetches(u_hbm, ubuf, sems, 1, chunks)
    for copy in copies:
        copy.start()
    for layer in range(2):
        for j in range(NJ):
            source = gyd_a if j < 2 else gyu_a
            gxd[pl.ds(gx_at(layer, j), HALF), :] = source[pl.ds(gy_at(j, layer), HALF), :]
            gxu[pl.ds(gx_at(layer, j), HALF), :] = source[pl.ds(gy_at(j, NI - 2 + layer), HALF), :]
            gxd[pl.ds(GX_ROWS + layer * NJ + j, 1), :] = source[
                pl.ds(GY_ROWS + (j % 2) * NI + layer, 1), :
            ]
            gxu[pl.ds(GX_ROWS + layer * NJ + j, 1), :] = source[
                pl.ds(GY_ROWS + (j % 2) * NI + NI - 2 + layer, 1), :
            ]
    for k in range(chunks):
        copies[k].wait()
        start, stop = k * HALF // chunks, (k + 1) * HALF // chunks
        turn(ubuf, turned, start, stop)
        for first in range(start, stop, 8):
            for i in range(NI):
                for j in range(NJ):
                    tile = turned[pl.ds(first * PITCH + i * NJ + j, 8, stride=PITCH), :]
                    (gyd if j < 2 else gyu)[pl.ds(gy_at(j, i) + first, 8), :] = tile
                    if i < 2:
                        gxd[pl.ds(gx_at(i, j) + HALF + first, 8), :] = tile
                    if i >= NI - 2:
                        gxu[pl.ds(gx_at(i - NI + 2, j) + HALF + first, 8), :] = tile


def local_kernel(gyd_a, gyu_a, gyd_b, gyu_b, hxm, hxp, visc, vel, out):
    lanes = lax.broadcasted_iota(jnp.int32, (8, NZ), 1)
    lane_row = lax.broadcasted_iota(jnp.int32, (1, NZ), 1)
    halves = ((gyd_a, gyu_a), (gyd_b, gyu_b))

    def load(i, j, first):
        if i < 0:
            return hxm[pl.ds(gx_at(i + 2, j) + first, 8), :]
        if i >= NI:
            return hxp[pl.ds(gx_at(i - NI, j) + first, 8), :]
        return halves[first // HALF][j // 2][pl.ds(gy_at(j, i) + first % HALF, 8), :]

    def nu(i, j):
        if i < 0:
            return hxm[pl.ds(GX_ROWS + (i + 2) * NJ + j, 1), :]
        if i >= NI:
            return hxp[pl.ds(GX_ROWS + (i - NI) * NJ + j, 1), :]
        return visc[pl.ds(i * NJ + j, 1), :]

    def wide(row):
        return jnp.broadcast_to(row, (8, NZ))

    for i in range(NI):
        for j in range(NJ):
            mid = nu(i, j)
            vx, vy, vz = (vel[pl.ds(d * CELLS + i * NJ + j, 1), :] for d in range(3))
            ax8, ax1 = wide(vx * (8.0 / 12.0)), wide(vx * (1.0 / 12.0))
            az8, az1 = wide(vz * (8.0 / 12.0)), wide(vz * (1.0 / 12.0))
            ay8 = wide(vy * (8.0 / 12.0))
            xp, xm = wide(0.5 * (mid + nu(i + 1, j))), wide(0.5 * (mid + nu(i - 1, j)))
            nz_up = jnp.where(lane_row == NZ - 1, 0.0, pltpu.roll(mid, NZ - 1, 1))
            nz_dn = jnp.where(lane_row == 0, 0.0, pltpu.roll(mid, 1, 1))
            zp, zm = wide(0.5 * (mid + nz_up)), wide(0.5 * (mid + nz_dn))
            yp = wide(0.5 * (mid + nu(i, j + 1))) if j < NJ - 1 else None
            ym = wide(0.5 * (mid + nu(i, j - 1))) if j > 0 else None
            for first in range(0, SN, 8):
                u = load(i, j, first)
                p1, m1 = load(i + 1, j, first), load(i - 1, j, first)
                p2, m2 = load(i + 2, j, first), load(i - 2, j, first)
                total = ax8 * (p1 - m1) - ax1 * (p2 - m2)
                total = total - (xp * (p1 - u) - xm * (u - m1))
                p1 = jnp.where(lanes == NZ - 1, 0.0, pltpu.roll(u, NZ - 1, 1))
                p2 = jnp.where(lanes >= NZ - 2, 0.0, pltpu.roll(u, NZ - 2, 1))
                m1 = jnp.where(lanes == 0, 0.0, pltpu.roll(u, 1, 1))
                m2 = jnp.where(lanes < 2, 0.0, pltpu.roll(u, 2, 1))
                total = total + (az8 * (p1 - m1) - az1 * (p2 - m2))
                total = total - (zp * (p1 - u) - zm * (u - m1))
                if j < NJ - 1:
                    p1 = load(i, j + 1, first)
                    total = total - yp * (p1 - u)
                if j > 0:
                    m1 = load(i, j - 1, first)
                    total = total + ym * (u - m1)
                if 0 < j < NJ - 1:
                    total = total + ay8 * (p1 - m1)
                out[(i * NJ + j) * SN + first : (i * NJ + j) * SN + first + 8, :] = total


def finish(half, base, gyd, gyu, hym, hyp, edge_m, edge_p, visc, vel, split, i):
    def wide(row):
        return jnp.broadcast_to(row, (16, NZ))

    vy = [vel[pl.ds(CELLS + i * NJ + j, 1), :] for j in range(NJ)]
    a8 = [wide(v * (8.0 / 12.0)) for v in vy]
    a1 = [wide(v * (1.0 / 12.0)) for v in vy]
    ym = wide(0.5 * (visc[pl.ds(i * NJ, 1), :] + edge_m[pl.ds(GY_ROWS + NI + i, 1), :]))
    yp = wide(0.5 * (visc[pl.ds(i * NJ + 3, 1), :] + edge_p[pl.ds(GY_ROWS + i, 1), :]))
    for first in range(0, HALF, 16):

        def at(ref, j, first=first):
            return ref[pl.ds(gy_at(j, i) + first, 16), :]

        u0, u1, u2, u3 = at(gyd, 0), at(gyd, 1), at(gyu, 2), at(gyu, 3)
        m2, m1, p1, p2 = at(hym, 0), at(hym, 1), at(hyp, 0), at(hyp, 1)
        adds = [
            (a8[0] * (u1 - m1) - a1[0] * (u2 - m2)) + ym * (u0 - m1),
            -a1[1] * (u3 - m1),
            -a1[2] * (p1 - u0),
            (a8[3] * (p1 - u2) - a1[3] * (p2 - u1)) - yp * (p1 - u3),
        ]
        for j in range(NJ):
            cell = i * NJ + j
            value = base[pl.ds(cell * SN + half * HALF + first, 16), :] + adds[j]
            high = value.astype(BF16)
            low = (value - high.astype(F32)).astype(BF16)
            split[first : first + 16, cell * NZ : (cell + 1) * NZ] = high
            split[HALF + first : HALF + first + 16, cell * NZ : (cell + 1) * NZ] = low


def over_cells(left, right):
    return lax.dot_general(left, right, (((1,), (1,)), ((), ())), preferred_element_type=F32)


def first_gram_kernel(base, gyd, gyu, hym, hyp, visc, vel, split, acc):
    for i in range(NI):
        finish(0, base, gyd, gyu, hym, hyp, hym, hyp, visc, vel, split, i)
        part = split[:, i * NJ * NZ : (i + 1) * NJ * NZ]
        fresh = over_cells(part, part)
        acc[...] = fresh if i == 0 else acc[...] + fresh


def second_gram_kernel(
    scale, base, gyd, gyu, hym, hyp, edge_m, edge_p, visc, vel, other, acc_a, split, gram, acc
):
    for i in range(NI):
        finish(1, base, gyd, gyu, hym, hyp, edge_m, edge_p, visc, vel, split, i)
        span = slice(i * NJ * NZ, (i + 1) * NJ * NZ)
        mine = split[:, span]
        fresh = over_cells(mine, jnp.concatenate([other[:, span], mine], axis=0))
        acc[...] = fresh if i == 0 else acc[...] + fresh

    def fold(block):
        rows = block[:HALF] + block[HALF:]
        return (rows[:, :HALF] + rows[:, HALF:]) * scale

    corner, cross, last = fold(acc_a[...]), fold(acc[:, :SN]), fold(acc[:, SN:])
    gram[:HALF, :] = jnp.concatenate([corner, cross.T], axis=1)
    gram[HALF:, :] = jnp.concatenate([cross, last], axis=1)


def spread_lane(row, lane):
    return jnp.take_along_axis(row, jnp.full((8, SN), lane, jnp.int32), axis=1)


def eliminate(work, upper, inverse, start, stop):
    lanes = lax.broadcasted_iota(jnp.int32, (8, SN), 1)
    width = BLOCK
    for base in range(start, stop, width):
        rows = [jnp.broadcast_to(work[base + k : base + k + 1, :], (8, SN)) for k in range(width)]
        entry = {}
        for r in range(width):
            for c in range(r + 1):
                entry[r, c] = spread_lane(rows[c], base + r)
        lower, inv, root = {}, {}, {}
        for k in range(width):
            inv[k] = 1.0 / entry[k, k]
            root[k] = lax.rsqrt(entry[k, k])
            for r in range(k + 1, width):
                lower[r, k] = entry[r, k] * inv[k]
                for c in range(k + 1, r + 1):
                    entry[r, c] = entry[r, c] - lower[r, k] * entry[c, k]
        inside = (lanes >= base) & (lanes < base + width)
        fwd, fwd_u, back = {}, {}, {}
        for k in range(width):
            z = jnp.where(inside, jnp.where(lanes == base + k, 1.0, 0.0), rows[k])
            zu = rows[k]
            for m in range(k):
                z = z - lower[k, m] * fwd[m]
                zu = zu - lower[k, m] * fwd_u[m]
            fwd[k], fwd_u[k] = z, zu
            upper[base + k : base + k + 1, :] = jnp.where(lanes >= base + k, zu * root[k], 0.0)[:1]
            inverse[base + k : base + k + 1, :] = jnp.where(lanes <= base + k, z * root[k], 0.0)[:1]
        first = base + width
        if first < SN:
            tile = work[first : first + 8, :]
            fresh = jnp.where(inside, 0.0, tile)
            columns = {}
            for k in range(width):
                column = jnp.broadcast_to(tile[:, base + k : base + k + 1], (8, SN))
                for m in range(k):
                    column = column - lower[k, m] * columns[m]
                columns[k] = column
                fresh = fresh - column * (fwd[k] * inv[k])
            work[first : first + 8, :] = fresh
        for k in reversed(range(width)):
            y = fwd[k] * inv[k]
            for m in range(k + 1, width):
                y = y - lower[m, k] * back[m]
            back[k] = y
        for top in range(first + 8, SN, 8):
            tile = work[top : top + 8, :]
            fresh = jnp.where(inside, 0.0, tile)
            for k in range(width):
                column = jnp.broadcast_to(tile[:, base + k : base + k + 1], (8, SN))
                fresh = fresh - column * back[k]
            work[top : top + 8, :] = fresh


def parts(value):
    high = value.astype(BF16)
    return high, (value - high.astype(F32)).astype(BF16)


def solve_kernel(gram, split_a, split_b, modes, upper, work, inverse, spread, done, sems):
    work[...] = gram[...]

    def put(half, left, right):
        for cell in range(0, CELLS, 2):
            product = jnp.dot(
                left, right(slice(cell * NZ, (cell + 2) * NZ)), preferred_element_type=F32
            )
            total = product[:HALF] + product[HALF:]
            top = half * HALF * PITCH + cell
            spread[pl.ds(top, HALF, stride=PITCH), :] = total[:, :NZ]
            spread[pl.ds(top + 1, HALF, stride=PITCH), :] = total[:, NZ:]
        for snap in range(half * HALF, (half + 1) * HALF):
            done[snap * CELLS : (snap + 1) * CELLS, :] = spread[
                snap * PITCH : snap * PITCH + CELLS, :
            ].astype(BF16)
        rows = pl.ds(half * (ROWS // 2), ROWS // 2)
        copy = pltpu.make_async_copy(done.at[rows], modes.at[rows], sems.at[half])
        copy.start()
        return copy

    eliminate(work, upper, inverse, 0, HALF)
    square = inverse[:HALF, :]
    high, low = parts(square + pltpu.roll(square, HALF, 1))
    copy_a = put(0, jnp.concatenate([high, low], axis=0), lambda span: split_a[:, span])
    eliminate(work, upper, inverse, HALF, SN)
    high, low = parts(inverse[HALF:, :])
    high, low = jnp.concatenate([high, high], axis=1), jnp.concatenate([low, low], axis=1)

    def both(span):
        return jnp.concatenate(
            [split_a[:HALF, span], split_b[:HALF, span], split_a[HALF:, span], split_b[HALF:, span]],
            axis=0,
        )

    copy_b = put(1, jnp.concatenate([high, low], axis=0), both)
    copy_a.wait()
    copy_b.wait()


def shape(*dims, dtype=F32):
    return jax.ShapeDtypeStruct(dims, dtype)


def onchip(*dims, dtype=F32):
    return pltpu.VMEM(dims, dtype)


def far(*values):
    return [pltpu.with_memory_space_constraint(v, pltpu.HBM) for v in values]


def near(*values):
    return [pltpu.with_memory_space_constraint(v, pltpu.VMEM) for v in values]


def call(kernel, out_shape, inputs, scratch, flops, moved, out_specs=None):
    return pl.pallas_call(
        kernel,
        out_shape=out_shape,
        in_specs=[space for space, _ in inputs],
        out_specs=[VMEM] * len(out_shape) if out_specs is None else out_specs,
        scratch_shapes=scratch,
        compiler_params=pltpu.CompilerParams(vmem_limit_bytes=LIMIT),
        cost_estimate=pl.CostEstimate(flops=flops, bytes_accessed=moved, transcendentals=0),
    )(*(value for _, value in inputs))


def whole_gram(gram):
    peers_y, peers_x = lax.axis_size("gy"), lax.axis_size("gx")
    rows = SN // peers_y
    pieces = lax.all_to_all(gram.reshape(peers_y, rows, SN), "gy", 0, 0)
    mine = jnp.sum(pieces, axis=0)
    pieces = lax.all_to_all(jnp.broadcast_to(mine[None], (peers_x, rows, SN)), "gx", 0, 0)
    mine = jnp.sum(pieces, axis=0)
    pieces = lax.all_to_all(jnp.broadcast_to(mine[None], (peers_y, rows, SN)), "gy", 0, 0)
    return pieces.reshape(SN, SN)


def per_device(snapshots, viscosity, velocity):
    flat = snapshots.reshape(ROWS, NZ)
    visc = viscosity.reshape(CELLS, NZ)
    vel = velocity.reshape(3 * CELLS, NZ)

    def vm(*values):
        return [(VMEM, value) for value in near(*values)]

    def hb(*values):
        return [(ANY, value) for value in far(*values)]

    def shifted(value, axis, step):
        peers = lax.axis_size(axis)
        pairs = [(k, k + step) for k in range(peers) if 0 <= k + step < peers]
        return lax.ppermute(value, axis, pairs)

    buffers = [pltpu.VMEM((ROWS // 2, NZ), F32), pltpu.VMEM((HALF * PITCH, NZ), F32)]
    gyd_a, gyu_a = call(
        first_pack_kernel,
        [onchip(GY_ROWS + 2 * NI, NZ)] * 2,
        hb(flat, visc),
        buffers + [pltpu.VMEM((CELLS, NZ), F32), pltpu.SemaphoreType.DMA((3,))],
        0,
        3 << 20,
    )
    hym_a, hyp_a = shifted(gyu_a, "gy", 1), shifted(gyd_a, "gy", -1)
    gyd_b, gyu_b, gxd, gxu = call(
        second_pack_kernel,
        [onchip(GY_ROWS, NZ)] * 2 + [onchip(GX_ROWS + 2 * NJ, NZ)] * 2,
        hb(flat) + vm(gyd_a, gyu_a),
        buffers + [pltpu.SemaphoreType.DMA((2,))],
        0,
        3 << 20,
    )
    hym_b, hyp_b = shifted(gyu_b, "gy", 1), shifted(gyd_b, "gy", -1)
    hxm, hxp = shifted(gxu, "gx", 1), shifted(gxd, "gx", -1)
    small = [(VMEM, visc), (VMEM, vel)]
    (base,) = call(
        local_kernel,
        [onchip(ROWS, NZ)],
        vm(gyd_a, gyu_a, gyd_b, gyu_b, hxm, hxp) + small,
        [],
        40 * ROWS * NZ,
        5 << 20,
    )
    count_cells = CELLS * NZ * lax.axis_size("gx") * lax.axis_size("gy")
    split_a, acc_a = call(
        first_gram_kernel,
        [onchip(SN, CELLS * NZ, dtype=BF16), onchip(SN, SN)],
        vm(base, gyd_a, gyu_a, hym_a, hyp_a) + small,
        [],
        2 * SN * SN * CELLS * NZ,
        4 << 20,
    )
    split_b, gram = call(
        functools.partial(second_gram_kernel, 1.0 / count_cells),
        [onchip(SN, CELLS * NZ, dtype=BF16), onchip(SN, SN)],
        vm(base, gyd_b, gyu_b, hym_b, hyp_b, hym_a, hyp_a) + small + vm(split_a, acc_a),
        [pltpu.VMEM((SN, 2 * SN), F32)],
        4 * SN * SN * CELLS * NZ,
        5 << 20,
    )
    total = whole_gram(gram)
    modes, factor = call(
        solve_kernel,
        [shape(ROWS, NZ, dtype=BF16), shape(SN, SN)],
        vm(total, split_a, split_b),
        [
            pltpu.VMEM((SN, SN), F32),
            pltpu.VMEM((SN, SN), F32),
            pltpu.VMEM((SN * PITCH, NZ), F32),
            pltpu.VMEM((ROWS, NZ), BF16),
            pltpu.SemaphoreType.DMA((2,)),
        ],
        8 * SN * SN * CELLS * NZ,
        4 << 20,
        [ANY, VMEM],
    )
    return modes.reshape(SN, NI, NJ, NZ), factor


def solution(mesh):
    placed = (P(None, "gx", "gy", None), P("gx", "gy", None), P(None, "gx", "gy", None))
    return jax.shard_map(
        per_device,
        mesh=mesh,
        in_specs=placed,
        out_specs=(P(None, "gx", "gy", None), P()),
        check_vma=False,
    )
```

```python
import functools

import jax
import jax.numpy as jnp
from jax import lax
from jax.experimental import pallas as pl
from jax.experimental.pallas import tpu as pltpu
from jax.sharding import PartitionSpec as P

F32 = jnp.float32
BF16 = jnp.bfloat16
SN, NI, NJ, NZ = 128, 8, 4, 128
CELLS = NI * NJ
ROWS = SN * CELLS
GY_ROWS = 2 * NI * SN
GX_ROWS = 2 * NJ * SN
BLOCK = 8
PITCH = CELLS + 1
LIMIT = 20 << 20
VMEM = pl.BlockSpec(memory_space=pltpu.VMEM)
ANY = pl.BlockSpec(memory_space=pl.ANY)


def gy_at(j, i):
    return ((j % 2) * NI + i) * SN


def gx_at(layer, j):
    return (layer * NJ + j) * SN


def pack_kernel(u_hbm, visc_hbm, gyd, gyu, gxd, gxu, ubuf, turned, visc, sems):
    chunks = 4
    small = pltpu.make_async_copy(visc_hbm, visc, sems.at[chunks])
    rows = ROWS // chunks
    copies = [
        pltpu.make_async_copy(
            u_hbm.at[pl.ds(k * rows, rows)], ubuf.at[pl.ds(k * rows, rows)], sems.at[k]
        )
        for k in range(chunks)
    ]
    for copy in copies:
        copy.start()
    small.start()
    for k in range(chunks):
        copies[k].wait()
        for snap in range(k * SN // chunks, (k + 1) * SN // chunks):
            for part in range(0, CELLS, 8):
                turned[snap * PITCH + part : snap * PITCH + part + 8, :] = ubuf[
                    snap * CELLS + part : snap * CELLS + part + 8, :
                ]
        for first in range(k * SN // chunks, (k + 1) * SN // chunks, 8):
            for i in range(NI):
                for j in range(NJ):
                    tile = turned[pl.ds(first * PITCH + i * NJ + j, 8, stride=PITCH), :]
                    (gyd if j < 2 else gyu)[pl.ds(gy_at(j, i) + first, 8), :] = tile
                    if i < 2:
                        gxd[pl.ds(gx_at(i, j) + first, 8), :] = tile
                    if i >= 6:
                        gxu[pl.ds(gx_at(i - 6, j) + first, 8), :] = tile
    small.wait()
    for i in range(NI):
        for j in range(NJ):
            row = visc[pl.ds(i * NJ + j, 1), :]
            (gyd if j < 2 else gyu)[pl.ds(GY_ROWS + (j % 2) * NI + i, 1), :] = row
            if i < 2:
                gxd[pl.ds(GX_ROWS + i * NJ + j, 1), :] = row
            if i >= 6:
                gxu[pl.ds(GX_ROWS + (i - 6) * NJ + j, 1), :] = row


def local_kernel(gyd, gyu, hxm, hxp, visc, vel, out):
    lanes = lax.broadcasted_iota(jnp.int32, (8, NZ), 1)
    lane_row = lax.broadcasted_iota(jnp.int32, (1, NZ), 1)

    def source(i, j):
        if i < 0:
            return hxm, gx_at(i + 2, j)
        if i >= NI:
            return hxp, gx_at(i - NI, j)
        return (gyd if j < 2 else gyu), gy_at(j, i)

    def nu(i, j):
        if i < 0:
            return hxm[pl.ds(GX_ROWS + (i + 2) * NJ + j, 1), :]
        if i >= NI:
            return hxp[pl.ds(GX_ROWS + (i - NI) * NJ + j, 1), :]
        return visc[pl.ds(i * NJ + j, 1), :]

    def wide(row):
        return jnp.broadcast_to(row, (8, NZ))

    for i in range(NI):
        for j in range(NJ):
            mid = nu(i, j)
            vx, vy, vz = (vel[pl.ds(d * CELLS + i * NJ + j, 1), :] for d in range(3))
            ax8, ax1 = wide(vx * (8.0 / 12.0)), wide(vx * (1.0 / 12.0))
            az8, az1 = wide(vz * (8.0 / 12.0)), wide(vz * (1.0 / 12.0))
            ay8 = wide(vy * (8.0 / 12.0))
            xp, xm = wide(0.5 * (mid + nu(i + 1, j))), wide(0.5 * (mid + nu(i - 1, j)))
            nz_up = jnp.where(lane_row == NZ - 1, 0.0, pltpu.roll(mid, NZ - 1, 1))
            nz_dn = jnp.where(lane_row == 0, 0.0, pltpu.roll(mid, 1, 1))
            zp, zm = wide(0.5 * (mid + nz_up)), wide(0.5 * (mid + nz_dn))
            yp = wide(0.5 * (mid + nu(i, j + 1))) if j < NJ - 1 else None
            ym = wide(0.5 * (mid + nu(i, j - 1))) if j > 0 else None

            def group(g, carry, i=i, j=j):
                first = g * 8

                def load(ii, jj):
                    ref, base = source(ii, jj)
                    return ref[pl.ds(base + first, 8), :]

                u = load(i, j)
                p1, m1, p2, m2 = load(i + 1, j), load(i - 1, j), load(i + 2, j), load(i - 2, j)
                total = ax8 * (p1 - m1) - ax1 * (p2 - m2)
                total = total - (xp * (p1 - u) - xm * (u - m1))
                p1 = jnp.where(lanes == NZ - 1, 0.0, pltpu.roll(u, NZ - 1, 1))
                p2 = jnp.where(lanes >= NZ - 2, 0.0, pltpu.roll(u, NZ - 2, 1))
                m1 = jnp.where(lanes == 0, 0.0, pltpu.roll(u, 1, 1))
                m2 = jnp.where(lanes < 2, 0.0, pltpu.roll(u, 2, 1))
                total = total + (az8 * (p1 - m1) - az1 * (p2 - m2))
                total = total - (zp * (p1 - u) - zm * (u - m1))
                if j < NJ - 1:
                    p1 = load(i, j + 1)
                    total = total - yp * (p1 - u)
                if j > 0:
                    m1 = load(i, j - 1)
                    total = total + ym * (u - m1)
                if 0 < j < NJ - 1:
                    total = total + ay8 * (p1 - m1)
                out[pl.ds((i * NJ + j) * SN + first, 8), :] = total
                return carry

            for g in range(SN // 8):
                group(g, 0)


def gram_kernel(scale, base, gyd, gyu, hym, hyp, visc, vel, split, gram, acc):
    acc[...] = jnp.zeros_like(acc)

    def wide(row):
        return jnp.broadcast_to(row, (16, NZ))

    for i in range(NI):
        mids = [visc[pl.ds(i * NJ + j, 1), :] for j in range(NJ)]
        vy = [vel[pl.ds(CELLS + i * NJ + j, 1), :] for j in range(NJ)]
        a8 = [wide(v * (8.0 / 12.0)) for v in vy]
        a1 = [wide(v * (1.0 / 12.0)) for v in vy]
        ym = wide(0.5 * (mids[0] + hym[pl.ds(GY_ROWS + NI + i, 1), :]))
        yp = wide(0.5 * (mids[3] + hyp[pl.ds(GY_ROWS + i, 1), :]))

        def group(g, carry, i=i, a8=a8, a1=a1, ym=ym, yp=yp):
            first = g * 16

            def at(ref, j):
                return ref[pl.ds(gy_at(j, i) + first, 16), :]

            u0, u1, u2, u3 = at(gyd, 0), at(gyd, 1), at(gyu, 2), at(gyu, 3)
            m2, m1, p1, p2 = at(hym, 0), at(hym, 1), at(hyp, 0), at(hyp, 1)
            adds = [
                (a8[0] * (u1 - m1) - a1[0] * (u2 - m2)) + ym * (u0 - m1),
                -a1[1] * (u3 - m1),
                -a1[2] * (p1 - u0),
                (a8[3] * (p1 - u2) - a1[3] * (p2 - u1)) - yp * (p1 - u3),
            ]
            for j in range(NJ):
                cell = i * NJ + j
                value = base[pl.ds(cell * SN + first, 16), :] + adds[j]
                high = value.astype(BF16)
                low = (value - high.astype(F32)).astype(BF16)
                split[pl.ds(first, 16), cell * NZ : (cell + 1) * NZ] = high
                split[pl.ds(SN + first, 16), cell * NZ : (cell + 1) * NZ] = low
            return carry

        for g in range(SN // 16):
            group(g, 0)
        part = split[:, i * NJ * NZ : (i + 1) * NJ * NZ]
        acc[...] += lax.dot_general(
            part, part, (((1,), (1,)), ((), ())), preferred_element_type=F32
        )
    gram[...] = (
        (acc[:SN, :SN] + acc[SN:, SN:]) + (acc[:SN, SN:] + acc[SN:, :SN])
    ) * scale


def spread_lane(row, lane):
    return jnp.take_along_axis(row, jnp.full((8, SN), lane, jnp.int32), axis=1)


def factorise(work, upper, inverse):
    lanes = lax.broadcasted_iota(jnp.int32, (8, SN), 1)
    width = BLOCK
    for base in range(0, SN, width):
        rows = [jnp.broadcast_to(work[base + k : base + k + 1, :], (8, SN)) for k in range(width)]
        entry = {}
        for r in range(width):
            for c in range(r + 1):
                entry[r, c] = spread_lane(rows[c], base + r)
        lower, inv, root = {}, {}, {}
        for k in range(width):
            inv[k] = 1.0 / entry[k, k]
            root[k] = lax.rsqrt(entry[k, k])
            for r in range(k + 1, width):
                lower[r, k] = entry[r, k] * inv[k]
                for c in range(k + 1, r + 1):
                    entry[r, c] = entry[r, c] - lower[r, k] * entry[c, k]
        inside = (lanes >= base) & (lanes < base + width)
        fwd, fwd_u, back = {}, {}, {}
        for k in range(width):
            z = jnp.where(inside, jnp.where(lanes == base + k, 1.0, 0.0), rows[k])
            zu = rows[k]
            for m in range(k):
                z = z - lower[k, m] * fwd[m]
                zu = zu - lower[k, m] * fwd_u[m]
            fwd[k], fwd_u[k] = z, zu
            upper[base + k : base + k + 1, :] = jnp.where(lanes >= base + k, zu * root[k], 0.0)[:1]
            inverse[base + k : base + k + 1, :] = jnp.where(lanes <= base + k, z * root[k], 0.0)[:1]
        first = base + width
        if first < SN:
            tile = work[first : first + 8, :]
            fresh = jnp.where(inside, 0.0, tile)
            columns = {}
            for k in range(width):
                column = jnp.broadcast_to(tile[:, base + k : base + k + 1], (8, SN))
                for m in range(k):
                    column = column - lower[k, m] * columns[m]
                columns[k] = column
                fresh = fresh - column * (fwd[k] * inv[k])
            work[first : first + 8, :] = fresh
        for k in reversed(range(width)):
            y = fwd[k] * inv[k]
            for m in range(k + 1, width):
                y = y - lower[m, k] * back[m]
            back[k] = y
        for top in range(first + 8, SN, 8):
            tile = work[top : top + 8, :]
            fresh = jnp.where(inside, 0.0, tile)
            for k in range(width):
                column = jnp.broadcast_to(tile[:, base + k : base + k + 1], (8, SN))
                fresh = fresh - column * back[k]
            work[top : top + 8, :] = fresh


def solve_kernel(gram, split, modes, upper, work, inverse, both, spread):
    work[...] = gram[...]
    factorise(work, upper, inverse)
    full = inverse[...]
    high = full.astype(BF16)
    low = (full - high.astype(F32)).astype(BF16)
    both[:SN, :SN] = high
    both[:SN, SN:] = high
    both[SN:, :SN] = low
    both[SN:, SN:] = low
    for cell in range(0, CELLS, 2):
        product = jnp.dot(
            both[...], split[:, cell * NZ : (cell + 2) * NZ], preferred_element_type=F32
        )
        total = product[:SN] + product[SN:]
        spread[pl.ds(cell, SN, stride=PITCH), :] = total[:, :NZ]
        spread[pl.ds(cell + 1, SN, stride=PITCH), :] = total[:, NZ:]
    for snap in range(SN):
        modes[snap * CELLS : (snap + 1) * CELLS, :] = spread[
            snap * PITCH : snap * PITCH + CELLS, :
        ].astype(BF16)


def shape(*dims, dtype=F32):
    return jax.ShapeDtypeStruct(dims, dtype)


def onchip(*dims, dtype=F32):
    return pltpu.VMEM(dims, dtype)


def far(*values):
    return [pltpu.with_memory_space_constraint(v, pltpu.HBM) for v in values]


def near(*values):
    return [pltpu.with_memory_space_constraint(v, pltpu.VMEM) for v in values]


def cost(flops, bytes_accessed):
    return pl.CostEstimate(flops=flops, bytes_accessed=bytes_accessed, transcendentals=0)


def whole_gram(gram):
    plane = 2 * lax.axis_size("gy")
    planes = lax.axis_size("gx") // 2
    within = [[k * plane + m for m in range(plane)] for k in range(planes)]
    across = [[k * plane + m for k in range(planes)] for m in range(plane)]
    rows = SN // plane

    def exchange(value, groups):
        return lax.all_to_all(value, ("gx", "gy"), 0, 0, axis_index_groups=groups)

    mine = jnp.sum(exchange(gram.reshape(plane, rows, SN), within), axis=0)
    mine = jnp.sum(exchange(jnp.broadcast_to(mine[None], (planes, rows, SN)), across), axis=0)
    pieces = exchange(jnp.broadcast_to(mine[None], (plane, rows, SN)), within)
    return pieces.reshape(SN, SN)


def per_device(snapshots, viscosity, velocity):
    flat = snapshots.reshape(ROWS, NZ)
    visc = viscosity.reshape(CELLS, NZ)
    vel = velocity.reshape(3 * CELLS, NZ)
    gyd, gyu, gxd, gxu = pl.pallas_call(
        pack_kernel,
        out_shape=(
            onchip(GY_ROWS + 2 * NI, NZ),
            onchip(GY_ROWS + 2 * NI, NZ),
            onchip(GX_ROWS + 2 * NJ, NZ),
            onchip(GX_ROWS + 2 * NJ, NZ),
        ),
        in_specs=[ANY, ANY],
        out_specs=[VMEM] * 4,
        scratch_shapes=[
            pltpu.VMEM((ROWS, NZ), F32),
            pltpu.VMEM((SN * PITCH, NZ), F32),
            pltpu.VMEM((CELLS, NZ), F32),
            pltpu.SemaphoreType.DMA((5,)),
        ],
        compiler_params=pltpu.CompilerParams(vmem_limit_bytes=LIMIT),
        cost_estimate=cost(0, 6 << 20),
    )(*far(flat, visc))

    def shifted(value, axis, step):
        peers = lax.axis_size(axis)
        pairs = [(k, k + step) for k in range(peers) if 0 <= k + step < peers]
        return lax.ppermute(value, axis, pairs)

    hym, hyp = shifted(gyu, "gy", 1), shifted(gyd, "gy", -1)
    hxm, hxp = shifted(gxu, "gx", 1), shifted(gxd, "gx", -1)
    base = pl.pallas_call(
        local_kernel,
        out_shape=onchip(ROWS, NZ),
        in_specs=[VMEM] * 6,
        out_specs=VMEM,
        compiler_params=pltpu.CompilerParams(vmem_limit_bytes=LIMIT),
        cost_estimate=cost(40 * ROWS * NZ, 5 << 20),
    )(*near(gyd, gyu, hxm, hxp), visc, vel)
    count_cells = CELLS * NZ * lax.axis_size("gx") * lax.axis_size("gy")
    split, gram = pl.pallas_call(
        functools.partial(gram_kernel, 1.0 / count_cells),
        out_shape=(onchip(2 * SN, CELLS * NZ, dtype=BF16), onchip(SN, SN)),
        in_specs=[VMEM] * 7,
        out_specs=[VMEM] * 2,
        scratch_shapes=[pltpu.VMEM((2 * SN, 2 * SN), F32)],
        compiler_params=pltpu.CompilerParams(vmem_limit_bytes=LIMIT),
        cost_estimate=cost(8 * SN * SN * CELLS * NZ, 8 << 20),
    )(*near(base, gyd, gyu, hym, hyp), visc, vel)
    total = whole_gram(gram)
    modes, factor = pl.pallas_call(
        solve_kernel,
        out_shape=(shape(ROWS, NZ, dtype=BF16), shape(SN, SN)),
        in_specs=[VMEM] * 2,
        out_specs=[VMEM] * 2,
        scratch_shapes=[
            pltpu.VMEM((SN, SN), F32),
            pltpu.VMEM((SN, SN), F32),
            pltpu.VMEM((2 * SN, 2 * SN), BF16),
            pltpu.VMEM((SN * PITCH, NZ), F32),
        ],
        compiler_params=pltpu.CompilerParams(vmem_limit_bytes=LIMIT),
        cost_estimate=cost(8 * SN * SN * CELLS * NZ, 4 << 20),
    )(*near(total, split))
    return modes.reshape(SN, NI, NJ, NZ), factor


def solution(mesh):
    placed = (P(None, "gx", "gy", None), P("gx", "gy", None), P(None, "gx", "gy", None))
    return jax.shard_map(
        per_device,
        mesh=mesh,
        in_specs=placed,
        out_specs=(P(None, "gx", "gy", None), P()),
        check_vma=False,
    )
```

```python
import functools

import jax
import jax.numpy as jnp
from jax import lax
from jax.experimental import pallas as pl
from jax.experimental.pallas import tpu as pltpu
from jax.sharding import PartitionSpec as P

F32 = jnp.float32
BF16 = jnp.bfloat16
SN, NI, NJ, NZ = 128, 8, 4, 128
CELLS = NI * NJ
ROWS = SN * CELLS
GY_ROWS = 2 * NI * SN
GX_ROWS = 2 * NJ * SN
BLOCK = 8
PITCH = CELLS + 1
LIMIT = 20 << 20
VMEM = pl.BlockSpec(memory_space=pltpu.VMEM)
ANY = pl.BlockSpec(memory_space=pl.ANY)


def gy_at(j, i):
    return ((j % 2) * NI + i) * SN


def gx_at(layer, j):
    return (layer * NJ + j) * SN


def pack_kernel(u_hbm, visc_hbm, gyd, gyu, gxd, gxu, ubuf, turned, visc, sems):
    chunks = 4
    small = pltpu.make_async_copy(visc_hbm, visc, sems.at[chunks])
    rows = ROWS // chunks
    copies = [
        pltpu.make_async_copy(
            u_hbm.at[pl.ds(k * rows, rows)], ubuf.at[pl.ds(k * rows, rows)], sems.at[k]
        )
        for k in range(chunks)
    ]
    for copy in copies:
        copy.start()
    small.start()
    for k in range(chunks):
        copies[k].wait()
        for snap in range(k * SN // chunks, (k + 1) * SN // chunks):
            for part in range(0, CELLS, 8):
                turned[snap * PITCH + part : snap * PITCH + part + 8, :] = ubuf[
                    snap * CELLS + part : snap * CELLS + part + 8, :
                ]
        for first in range(k * SN // chunks, (k + 1) * SN // chunks, 8):
            for i in range(NI):
                for j in range(NJ):
                    tile = turned[pl.ds(first * PITCH + i * NJ + j, 8, stride=PITCH), :]
                    (gyd if j < 2 else gyu)[pl.ds(gy_at(j, i) + first, 8), :] = tile
                    if i < 2:
                        gxd[pl.ds(gx_at(i, j) + first, 8), :] = tile
                    if i >= 6:
                        gxu[pl.ds(gx_at(i - 6, j) + first, 8), :] = tile
    small.wait()
    for i in range(NI):
        for j in range(NJ):
            row = visc[pl.ds(i * NJ + j, 1), :]
            (gyd if j < 2 else gyu)[pl.ds(GY_ROWS + (j % 2) * NI + i, 1), :] = row
            if i < 2:
                gxd[pl.ds(GX_ROWS + i * NJ + j, 1), :] = row
            if i >= 6:
                gxu[pl.ds(GX_ROWS + (i - 6) * NJ + j, 1), :] = row


def local_kernel(gyd, gyu, hxm, hxp, visc, vel, out):
    lanes = lax.broadcasted_iota(jnp.int32, (8, NZ), 1)
    lane_row = lax.broadcasted_iota(jnp.int32, (1, NZ), 1)

    def source(i, j):
        if i < 0:
            return hxm, gx_at(i + 2, j)
        if i >= NI:
            return hxp, gx_at(i - NI, j)
        return (gyd if j < 2 else gyu), gy_at(j, i)

    def nu(i, j):
        if i < 0:
            return hxm[pl.ds(GX_ROWS + (i + 2) * NJ + j, 1), :]
        if i >= NI:
            return hxp[pl.ds(GX_ROWS + (i - NI) * NJ + j, 1), :]
        return visc[pl.ds(i * NJ + j, 1), :]

    def wide(row):
        return jnp.broadcast_to(row, (8, NZ))

    for i in range(NI):
        for j in range(NJ):
            mid = nu(i, j)
            vx, vy, vz = (vel[pl.ds(d * CELLS + i * NJ + j, 1), :] for d in range(3))
            ax8, ax1 = wide(vx * (8.0 / 12.0)), wide(vx * (1.0 / 12.0))
            az8, az1 = wide(vz * (8.0 / 12.0)), wide(vz * (1.0 / 12.0))
            ay8 = wide(vy * (8.0 / 12.0))
            xp, xm = wide(0.5 * (mid + nu(i + 1, j))), wide(0.5 * (mid + nu(i - 1, j)))
            nz_up = jnp.where(lane_row == NZ - 1, 0.0, pltpu.roll(mid, NZ - 1, 1))
            nz_dn = jnp.where(lane_row == 0, 0.0, pltpu.roll(mid, 1, 1))
            zp, zm = wide(0.5 * (mid + nz_up)), wide(0.5 * (mid + nz_dn))
            yp = wide(0.5 * (mid + nu(i, j + 1))) if j < NJ - 1 else None
            ym = wide(0.5 * (mid + nu(i, j - 1))) if j > 0 else None

            def group(g, carry, i=i, j=j):
                first = g * 8

                def load(ii, jj):
                    ref, base = source(ii, jj)
                    return ref[pl.ds(base + first, 8), :]

                u = load(i, j)
                p1, m1, p2, m2 = load(i + 1, j), load(i - 1, j), load(i + 2, j), load(i - 2, j)
                total = ax8 * (p1 - m1) - ax1 * (p2 - m2)
                total = total - (xp * (p1 - u) - xm * (u - m1))
                p1 = jnp.where(lanes == NZ - 1, 0.0, pltpu.roll(u, NZ - 1, 1))
                p2 = jnp.where(lanes >= NZ - 2, 0.0, pltpu.roll(u, NZ - 2, 1))
                m1 = jnp.where(lanes == 0, 0.0, pltpu.roll(u, 1, 1))
                m2 = jnp.where(lanes < 2, 0.0, pltpu.roll(u, 2, 1))
                total = total + (az8 * (p1 - m1) - az1 * (p2 - m2))
                total = total - (zp * (p1 - u) - zm * (u - m1))
                if j < NJ - 1:
                    p1 = load(i, j + 1)
                    total = total - yp * (p1 - u)
                if j > 0:
                    m1 = load(i, j - 1)
                    total = total + ym * (u - m1)
                if 0 < j < NJ - 1:
                    total = total + ay8 * (p1 - m1)
                out[pl.ds((i * NJ + j) * SN + first, 8), :] = total
                return carry

            for g in range(SN // 8):
                group(g, 0)


def over_cells(value):
    return lax.dot_general(value, value, (((1,), (1,)), ((), ())), preferred_element_type=F32)


def put_split(split, value, first, column):
    high = value.astype(BF16)
    low = (value - high.astype(F32)).astype(BF16)
    split[first : first + 16, column : column + NZ] = high
    split[SN + first : SN + first + 16, column : column + NZ] = low


def upper_rows_kernel(base, gyd, gyu, hyp, visc, vel, split, acc):
    def wide(row):
        return jnp.broadcast_to(row, (16, NZ))

    for i in range(NI):
        vy = [vel[pl.ds(CELLS + i * NJ + j, 1), :] for j in range(NJ)]
        a8, a1, a1_in = wide(vy[3] * (8.0 / 12.0)), wide(vy[3] * (1.0 / 12.0)), wide(vy[2] * (1.0 / 12.0))
        yp = wide(0.5 * (visc[pl.ds(i * NJ + 3, 1), :] + hyp[pl.ds(GY_ROWS + i, 1), :]))
        for first in range(0, SN, 16):

            def at(ref, j, first=first):
                return ref[pl.ds(gy_at(j, i) + first, 16), :]

            u0, u1, u2, u3 = at(gyd, 0), at(gyd, 1), at(gyu, 2), at(gyu, 3)
            p1, p2 = at(hyp, 0), at(hyp, 1)
            row = (i * NJ + 2) * SN + first
            put_split(split, base[row : row + 16, :] - a1_in * (p1 - u0), first, i * 2 * NZ)
            edge = (a8 * (p1 - u2) - a1 * (p2 - u1)) - yp * (p1 - u3)
            put_split(split, base[row + SN : row + SN + 16, :] + edge, first, (i * 2 + 1) * NZ)
        fresh = over_cells(split[:, i * 2 * NZ : (i + 1) * 2 * NZ])
        acc[...] = fresh if i == 0 else acc[...] + fresh


def lower_rows_kernel(scale, base, gyd, gyu, hym, visc, vel, acc_up, split, gram, acc):
    def wide(row):
        return jnp.broadcast_to(row, (16, NZ))

    for i in range(NI):
        vy = [vel[pl.ds(CELLS + i * NJ + j, 1), :] for j in range(NJ)]
        a8, a1, a1_in = wide(vy[0] * (8.0 / 12.0)), wide(vy[0] * (1.0 / 12.0)), wide(vy[1] * (1.0 / 12.0))
        ym = wide(0.5 * (visc[pl.ds(i * NJ, 1), :] + hym[pl.ds(GY_ROWS + NI + i, 1), :]))
        for first in range(0, SN, 16):

            def at(ref, j, first=first):
                return ref[pl.ds(gy_at(j, i) + first, 16), :]

            u0, u1, u2, u3 = at(gyd, 0), at(gyd, 1), at(gyu, 2), at(gyu, 3)
            m2, m1 = at(hym, 0), at(hym, 1)
            row = i * NJ * SN + first
            edge = (a8 * (u1 - m1) - a1 * (u2 - m2)) + ym * (u0 - m1)
            put_split(split, base[row : row + 16, :] + edge, first, i * 2 * NZ)
            put_split(
                split, base[row + SN : row + SN + 16, :] - a1_in * (u3 - m1), first, (i * 2 + 1) * NZ
            )
        fresh = over_cells(split[:, i * 2 * NZ : (i + 1) * 2 * NZ])
        acc[...] = acc_up[...] + fresh if i == 0 else acc[...] + fresh
    gram[...] = (
        (acc[:SN, :SN] + acc[SN:, SN:]) + (acc[:SN, SN:] + acc[SN:, :SN])
    ) * scale


def spread_lane(row, lane):
    return jnp.take_along_axis(row, jnp.full((8, SN), lane, jnp.int32), axis=1)


def factorise(work, upper, inverse):
    lanes = lax.broadcasted_iota(jnp.int32, (8, SN), 1)
    width = BLOCK
    for base in range(0, SN, width):
        rows = [jnp.broadcast_to(work[base + k : base + k + 1, :], (8, SN)) for k in range(width)]
        entry = {}
        for r in range(width):
            for c in range(r + 1):
                entry[r, c] = spread_lane(rows[c], base + r)
        lower, inv, root = {}, {}, {}
        for k in range(width):
            inv[k] = 1.0 / entry[k, k]
            root[k] = lax.rsqrt(entry[k, k])
            for r in range(k + 1, width):
                lower[r, k] = entry[r, k] * inv[k]
                for c in range(k + 1, r + 1):
                    entry[r, c] = entry[r, c] - lower[r, k] * entry[c, k]
        inside = (lanes >= base) & (lanes < base + width)
        fwd, fwd_u, back = {}, {}, {}
        for k in range(width):
            z = jnp.where(inside, jnp.where(lanes == base + k, 1.0, 0.0), rows[k])
            zu = rows[k]
            for m in range(k):
                z = z - lower[k, m] * fwd[m]
                zu = zu - lower[k, m] * fwd_u[m]
            fwd[k], fwd_u[k] = z, zu
            upper[base + k : base + k + 1, :] = jnp.where(lanes >= base + k, zu * root[k], 0.0)[:1]
            inverse[base + k : base + k + 1, :] = jnp.where(lanes <= base + k, z * root[k], 0.0)[:1]
        first = base + width
        if first < SN:
            tile = work[first : first + 8, :]
            fresh = jnp.where(inside, 0.0, tile)
            columns = {}
            for k in range(width):
                column = jnp.broadcast_to(tile[:, base + k : base + k + 1], (8, SN))
                for m in range(k):
                    column = column - lower[k, m] * columns[m]
                columns[k] = column
                fresh = fresh - column * (fwd[k] * inv[k])
            work[first : first + 8, :] = fresh
        for k in reversed(range(width)):
            y = fwd[k] * inv[k]
            for m in range(k + 1, width):
                y = y - lower[m, k] * back[m]
            back[k] = y
        for top in range(first + 8, SN, 8):
            tile = work[top : top + 8, :]
            fresh = jnp.where(inside, 0.0, tile)
            for k in range(width):
                column = jnp.broadcast_to(tile[:, base + k : base + k + 1], (8, SN))
                fresh = fresh - column * back[k]
            work[top : top + 8, :] = fresh


def solve_kernel(grams, split_m, split_p, modes, upper, work, inverse, both, spread):
    work[...] = grams[:SN, :] + grams[SN:, :]
    factorise(work, upper, inverse)
    full = inverse[...]
    high = full.astype(BF16)
    low = (full - high.astype(F32)).astype(BF16)
    both[:SN, :SN] = high
    both[:SN, SN:] = high
    both[SN:, :SN] = low
    both[SN:, SN:] = low
    for cell in range(0, CELLS, 2):
        split = split_m if cell % NJ == 0 else split_p
        column = cell // NJ * 2 * NZ
        product = jnp.dot(
            both[...], split[:, column : column + 2 * NZ], preferred_element_type=F32
        )
        total = product[:SN] + product[SN:]
        spread[pl.ds(cell, SN, stride=PITCH), :] = total[:, :NZ]
        spread[pl.ds(cell + 1, SN, stride=PITCH), :] = total[:, NZ:]
    for snap in range(SN):
        modes[snap * CELLS : (snap + 1) * CELLS, :] = spread[
            snap * PITCH : snap * PITCH + CELLS, :
        ].astype(BF16)


def shape(*dims, dtype=F32):
    return jax.ShapeDtypeStruct(dims, dtype)


def onchip(*dims, dtype=F32):
    return pltpu.VMEM(dims, dtype)


def far(*values):
    return [pltpu.with_memory_space_constraint(v, pltpu.HBM) for v in values]


def near(*values):
    return [pltpu.with_memory_space_constraint(v, pltpu.VMEM) for v in values]


def cost(flops, bytes_accessed):
    return pl.CostEstimate(flops=flops, bytes_accessed=bytes_accessed, transcendentals=0)


def plane_grams(gram):
    peers = lax.axis_size("gy")
    plane = 2 * peers
    planes = lax.axis_size("gx") // 2
    within = [[k * plane + m for m in range(plane)] for k in range(planes)]
    across = [[k * plane + m for k in range(planes)] for m in range(plane)]
    rows = SN // peers

    def exchange(value, groups):
        return lax.all_to_all(value, ("gx", "gy"), 0, 0, axis_index_groups=groups)

    mine = jnp.sum(lax.all_to_all(gram.reshape(peers, rows, SN), "gy", 0, 0), axis=0)
    mine = jnp.sum(exchange(jnp.broadcast_to(mine[None], (planes, rows, SN)), across), axis=0)
    pieces = exchange(jnp.broadcast_to(mine[None], (plane, rows, SN)), within)
    return pieces.reshape(2 * SN, SN)


def per_device(snapshots, viscosity, velocity):
    flat = snapshots.reshape(ROWS, NZ)
    visc = viscosity.reshape(CELLS, NZ)
    vel = velocity.reshape(3 * CELLS, NZ)
    gyd, gyu, gxd, gxu = pl.pallas_call(
        pack_kernel,
        out_shape=(
            onchip(GY_ROWS + 2 * NI, NZ),
            onchip(GY_ROWS + 2 * NI, NZ),
            onchip(GX_ROWS + 2 * NJ, NZ),
            onchip(GX_ROWS + 2 * NJ, NZ),
        ),
        in_specs=[ANY, ANY],
        out_specs=[VMEM] * 4,
        scratch_shapes=[
            pltpu.VMEM((ROWS, NZ), F32),
            pltpu.VMEM((SN * PITCH, NZ), F32),
            pltpu.VMEM((CELLS, NZ), F32),
            pltpu.SemaphoreType.DMA((5,)),
        ],
        compiler_params=pltpu.CompilerParams(vmem_limit_bytes=LIMIT),
        cost_estimate=cost(0, 6 << 20),
    )(*far(flat, visc))

    def shifted(value, axis, step):
        peers = lax.axis_size(axis)
        pairs = [(k, k + step) for k in range(peers) if 0 <= k + step < peers]
        return lax.ppermute(value, axis, pairs)

    hym, hyp = shifted(gyu, "gy", 1), shifted(gyd, "gy", -1)
    hxm, hxp = shifted(gxu, "gx", 1), shifted(gxd, "gx", -1)
    base = pl.pallas_call(
        local_kernel,
        out_shape=onchip(ROWS, NZ),
        in_specs=[VMEM] * 6,
        out_specs=VMEM,
        compiler_params=pltpu.CompilerParams(vmem_limit_bytes=LIMIT),
        cost_estimate=cost(40 * ROWS * NZ, 5 << 20),
    )(*near(gyd, gyu, hxm, hxp), visc, vel)
    count_cells = CELLS * NZ * lax.axis_size("gx") * lax.axis_size("gy")
    split_p, acc_up = pl.pallas_call(
        upper_rows_kernel,
        out_shape=(onchip(2 * SN, CELLS * NZ // 2, dtype=BF16), onchip(2 * SN, 2 * SN)),
        in_specs=[VMEM] * 6,
        out_specs=[VMEM] * 2,
        compiler_params=pltpu.CompilerParams(vmem_limit_bytes=LIMIT),
        cost_estimate=cost(4 * SN * SN * CELLS * NZ, 4 << 20),
    )(*near(base, gyd, gyu, hyp), visc, vel)
    split_m, gram = pl.pallas_call(
        functools.partial(lower_rows_kernel, 1.0 / count_cells),
        out_shape=(onchip(2 * SN, CELLS * NZ // 2, dtype=BF16), onchip(SN, SN)),
        in_specs=[VMEM] * 7,
        out_specs=[VMEM] * 2,
        scratch_shapes=[pltpu.VMEM((2 * SN, 2 * SN), F32)],
        compiler_params=pltpu.CompilerParams(vmem_limit_bytes=LIMIT),
        cost_estimate=cost(4 * SN * SN * CELLS * NZ, 4 << 20),
    )(*near(base, gyd, gyu, hym), visc, vel, *near(acc_up))
    total = plane_grams(gram)
    modes, factor = pl.pallas_call(
        solve_kernel,
        out_shape=(shape(ROWS, NZ, dtype=BF16), shape(SN, SN)),
        in_specs=[VMEM] * 3,
        out_specs=[VMEM] * 2,
        scratch_shapes=[
            pltpu.VMEM((SN, SN), F32),
            pltpu.VMEM((SN, SN), F32),
            pltpu.VMEM((2 * SN, 2 * SN), BF16),
            pltpu.VMEM((SN * PITCH, NZ), F32),
        ],
        compiler_params=pltpu.CompilerParams(vmem_limit_bytes=LIMIT),
        cost_estimate=cost(8 * SN * SN * CELLS * NZ, 4 << 20),
    )(*near(total, split_m, split_p))
    return modes.reshape(SN, NI, NJ, NZ), factor


def solution(mesh):
    placed = (P(None, "gx", "gy", None), P("gx", "gy", None), P(None, "gx", "gy", None))
    return jax.shard_map(
        per_device,
        mesh=mesh,
        in_specs=placed,
        out_specs=(P(None, "gx", "gy", None), P()),
        check_vma=False,
    )
```

```python
import functools

import jax
import jax.numpy as jnp
from jax import lax
from jax.experimental import pallas as pl
from jax.experimental.pallas import tpu as pltpu
from jax.sharding import PartitionSpec as P

F32 = jnp.float32
BF16 = jnp.bfloat16
SN, NI, NJ, NZ = 128, 8, 4, 128
CELLS = NI * NJ
ROWS = SN * CELLS
GY_ROWS = 2 * NI * SN
GX_ROWS = 2 * NJ * SN
BLOCK = 8
PITCH = CELLS + 1
LIMIT = 20 << 20
VMEM = pl.BlockSpec(memory_space=pltpu.VMEM)
ANY = pl.BlockSpec(memory_space=pl.ANY)


def gy_at(j, i):
    return ((j % 2) * NI + i) * SN


def gx_at(layer, j):
    return (layer * NJ + j) * SN


def pack_kernel(u_hbm, visc_hbm, gyd, gyu, gxd, gxu, ubuf, turned, visc, sems):
    chunks = 4
    small = pltpu.make_async_copy(visc_hbm, visc, sems.at[chunks])
    rows = ROWS // chunks
    copies = [
        pltpu.make_async_copy(
            u_hbm.at[pl.ds(k * rows, rows)], ubuf.at[pl.ds(k * rows, rows)], sems.at[k]
        )
        for k in range(chunks)
    ]
    for copy in copies:
        copy.start()
    small.start()
    for k in range(chunks):
        copies[k].wait()
        for snap in range(k * SN // chunks, (k + 1) * SN // chunks):
            for part in range(0, CELLS, 8):
                turned[snap * PITCH + part : snap * PITCH + part + 8, :] = ubuf[
                    snap * CELLS + part : snap * CELLS + part + 8, :
                ]
        for first in range(k * SN // chunks, (k + 1) * SN // chunks, 8):
            for i in range(NI):
                for j in range(NJ):
                    tile = turned[pl.ds(first * PITCH + i * NJ + j, 8, stride=PITCH), :]
                    (gyd if j < 2 else gyu)[pl.ds(gy_at(j, i) + first, 8), :] = tile
                    if i < 2:
                        gxd[pl.ds(gx_at(i, j) + first, 8), :] = tile
                    if i >= 6:
                        gxu[pl.ds(gx_at(i - 6, j) + first, 8), :] = tile
    small.wait()
    for i in range(NI):
        for j in range(NJ):
            row = visc[pl.ds(i * NJ + j, 1), :]
            (gyd if j < 2 else gyu)[pl.ds(GY_ROWS + (j % 2) * NI + i, 1), :] = row
            if i < 2:
                gxd[pl.ds(GX_ROWS + i * NJ + j, 1), :] = row
            if i >= 6:
                gxu[pl.ds(GX_ROWS + (i - 6) * NJ + j, 1), :] = row


def local_kernel(gyd, gyu, hxm, hxp, visc, vel, out):
    lanes = lax.broadcasted_iota(jnp.int32, (8, NZ), 1)
    lane_row = lax.broadcasted_iota(jnp.int32, (1, NZ), 1)

    def source(i, j):
        if i < 0:
            return hxm, gx_at(i + 2, j)
        if i >= NI:
            return hxp, gx_at(i - NI, j)
        return (gyd if j < 2 else gyu), gy_at(j, i)

    def nu(i, j):
        if i < 0:
            return hxm[pl.ds(GX_ROWS + (i + 2) * NJ + j, 1), :]
        if i >= NI:
            return hxp[pl.ds(GX_ROWS + (i - NI) * NJ + j, 1), :]
        return visc[pl.ds(i * NJ + j, 1), :]

    def wide(row):
        return jnp.broadcast_to(row, (8, NZ))

    for i in range(NI):
        for j in range(NJ):
            mid = nu(i, j)
            vx, vy, vz = (vel[pl.ds(d * CELLS + i * NJ + j, 1), :] for d in range(3))
            ax8, ax1 = wide(vx * (8.0 / 12.0)), wide(vx * (1.0 / 12.0))
            az8, az1 = wide(vz * (8.0 / 12.0)), wide(vz * (1.0 / 12.0))
            ay8 = wide(vy * (8.0 / 12.0))
            xp, xm = wide(0.5 * (mid + nu(i + 1, j))), wide(0.5 * (mid + nu(i - 1, j)))
            nz_up = jnp.where(lane_row == NZ - 1, 0.0, pltpu.roll(mid, NZ - 1, 1))
            nz_dn = jnp.where(lane_row == 0, 0.0, pltpu.roll(mid, 1, 1))
            zp, zm = wide(0.5 * (mid + nz_up)), wide(0.5 * (mid + nz_dn))
            yp = wide(0.5 * (mid + nu(i, j + 1))) if j < NJ - 1 else None
            ym = wide(0.5 * (mid + nu(i, j - 1))) if j > 0 else None

            def group(g, carry, i=i, j=j):
                first = g * 8

                def load(ii, jj):
                    ref, base = source(ii, jj)
                    return ref[pl.ds(base + first, 8), :]

                u = load(i, j)
                p1, m1, p2, m2 = load(i + 1, j), load(i - 1, j), load(i + 2, j), load(i - 2, j)
                total = ax8 * (p1 - m1) - ax1 * (p2 - m2)
                total = total - (xp * (p1 - u) - xm * (u - m1))
                p1 = jnp.where(lanes == NZ - 1, 0.0, pltpu.roll(u, NZ - 1, 1))
                p2 = jnp.where(lanes >= NZ - 2, 0.0, pltpu.roll(u, NZ - 2, 1))
                m1 = jnp.where(lanes == 0, 0.0, pltpu.roll(u, 1, 1))
                m2 = jnp.where(lanes < 2, 0.0, pltpu.roll(u, 2, 1))
                total = total + (az8 * (p1 - m1) - az1 * (p2 - m2))
                total = total - (zp * (p1 - u) - zm * (u - m1))
                if j < NJ - 1:
                    p1 = load(i, j + 1)
                    total = total - yp * (p1 - u)
                if j > 0:
                    m1 = load(i, j - 1)
                    total = total + ym * (u - m1)
                if 0 < j < NJ - 1:
                    total = total + ay8 * (p1 - m1)
                out[pl.ds((i * NJ + j) * SN + first, 8), :] = total
                return carry

            for g in range(SN // 8):
                group(g, 0)


def over_cells(value):
    return lax.dot_general(value, value, (((1,), (1,)), ((), ())), preferred_element_type=F32)


def put_split(split, value, first, column):
    high = value.astype(BF16)
    low = (value - high.astype(F32)).astype(BF16)
    split[first : first + 16, column : column + NZ] = high
    split[SN + first : SN + first + 16, column : column + NZ] = low


def upper_rows_kernel(base, gyd, gyu, hyp, visc, vel, split, acc):
    def wide(row):
        return jnp.broadcast_to(row, (16, NZ))

    for i in range(NI):
        vy = [vel[pl.ds(CELLS + i * NJ + j, 1), :] for j in range(NJ)]
        a8, a1, a1_in = wide(vy[3] * (8.0 / 12.0)), wide(vy[3] * (1.0 / 12.0)), wide(vy[2] * (1.0 / 12.0))
        yp = wide(0.5 * (visc[pl.ds(i * NJ + 3, 1), :] + hyp[pl.ds(GY_ROWS + i, 1), :]))
        for first in range(0, SN, 16):

            def at(ref, j, first=first):
                return ref[pl.ds(gy_at(j, i) + first, 16), :]

            u0, u1, u2, u3 = at(gyd, 0), at(gyd, 1), at(gyu, 2), at(gyu, 3)
            p1, p2 = at(hyp, 0), at(hyp, 1)
            row = (i * NJ + 2) * SN + first
            put_split(split, base[row : row + 16, :] - a1_in * (p1 - u0), first, i * 2 * NZ)
            edge = (a8 * (p1 - u2) - a1 * (p2 - u1)) - yp * (p1 - u3)
            put_split(split, base[row + SN : row + SN + 16, :] + edge, first, (i * 2 + 1) * NZ)
        fresh = over_cells(split[:, i * 2 * NZ : (i + 1) * 2 * NZ])
        acc[...] = fresh if i == 0 else acc[...] + fresh


def lower_rows_kernel(scale, base, gyd, gyu, hym, visc, vel, acc_up, split, gram, acc):
    def wide(row):
        return jnp.broadcast_to(row, (16, NZ))

    for i in range(NI):
        vy = [vel[pl.ds(CELLS + i * NJ + j, 1), :] for j in range(NJ)]
        a8, a1, a1_in = wide(vy[0] * (8.0 / 12.0)), wide(vy[0] * (1.0 / 12.0)), wide(vy[1] * (1.0 / 12.0))
        ym = wide(0.5 * (visc[pl.ds(i * NJ, 1), :] + hym[pl.ds(GY_ROWS + NI + i, 1), :]))
        for first in range(0, SN, 16):

            def at(ref, j, first=first):
                return ref[pl.ds(gy_at(j, i) + first, 16), :]

            u0, u1, u2, u3 = at(gyd, 0), at(gyd, 1), at(gyu, 2), at(gyu, 3)
            m2, m1 = at(hym, 0), at(hym, 1)
            row = i * NJ * SN + first
            edge = (a8 * (u1 - m1) - a1 * (u2 - m2)) + ym * (u0 - m1)
            put_split(split, base[row : row + 16, :] + edge, first, i * 2 * NZ)
            put_split(
                split, base[row + SN : row + SN + 16, :] - a1_in * (u3 - m1), first, (i * 2 + 1) * NZ
            )
        fresh = over_cells(split[:, i * 2 * NZ : (i + 1) * 2 * NZ])
        acc[...] = acc_up[...] + fresh if i == 0 else acc[...] + fresh
    gram[...] = (
        (acc[:SN, :SN] + acc[SN:, SN:]) + (acc[:SN, SN:] + acc[SN:, :SN])
    ) * scale


def spread_lane(row, lane):
    return jnp.take_along_axis(row, jnp.full((8, SN), lane, jnp.int32), axis=1)


def factorise(work, upper, inverse):
    lanes = lax.broadcasted_iota(jnp.int32, (8, SN), 1)
    width = BLOCK
    for base in range(0, SN, width):
        rows = [jnp.broadcast_to(work[base + k : base + k + 1, :], (8, SN)) for k in range(width)]
        entry = {}
        for r in range(width):
            for c in range(r + 1):
                entry[r, c] = spread_lane(rows[c], base + r)
        lower, inv, root = {}, {}, {}
        for k in range(width):
            inv[k] = 1.0 / entry[k, k]
            root[k] = lax.rsqrt(entry[k, k])
            for r in range(k + 1, width):
                lower[r, k] = entry[r, k] * inv[k]
                for c in range(k + 1, r + 1):
                    entry[r, c] = entry[r, c] - lower[r, k] * entry[c, k]
        inside = (lanes >= base) & (lanes < base + width)
        fwd, fwd_u, back = {}, {}, {}
        for k in range(width):
            z = jnp.where(inside, jnp.where(lanes == base + k, 1.0, 0.0), rows[k])
            zu = rows[k]
            for m in range(k):
                z = z - lower[k, m] * fwd[m]
                zu = zu - lower[k, m] * fwd_u[m]
            fwd[k], fwd_u[k] = z, zu
            upper[base + k : base + k + 1, :] = jnp.where(lanes >= base + k, zu * root[k], 0.0)[:1]
            inverse[base + k : base + k + 1, :] = jnp.where(lanes <= base + k, z * root[k], 0.0)[:1]
        first = base + width
        if first < SN:
            tile = work[first : first + 8, :]
            fresh = jnp.where(inside, 0.0, tile)
            columns = {}
            for k in range(width):
                column = jnp.broadcast_to(tile[:, base + k : base + k + 1], (8, SN))
                for m in range(k):
                    column = column - lower[k, m] * columns[m]
                columns[k] = column
                fresh = fresh - column * (fwd[k] * inv[k])
            work[first : first + 8, :] = fresh
        for k in reversed(range(width)):
            y = fwd[k] * inv[k]
            for m in range(k + 1, width):
                y = y - lower[m, k] * back[m]
            back[k] = y
        for top in range(first + 8, SN, 8):
            tile = work[top : top + 8, :]
            fresh = jnp.where(inside, 0.0, tile)
            for k in range(width):
                column = jnp.broadcast_to(tile[:, base + k : base + k + 1], (8, SN))
                fresh = fresh - column * back[k]
            work[top : top + 8, :] = fresh


def solve_kernel(gram, split_m, split_p, modes, upper, work, inverse, both, spread):
    work[...] = gram[...]
    factorise(work, upper, inverse)
    full = inverse[...]
    high = full.astype(BF16)
    low = (full - high.astype(F32)).astype(BF16)
    both[:SN, :SN] = high
    both[:SN, SN:] = high
    both[SN:, :SN] = low
    both[SN:, SN:] = low
    for cell in range(0, CELLS, 2):
        split = split_m if cell % NJ == 0 else split_p
        column = cell // NJ * 2 * NZ
        product = jnp.dot(
            both[...], split[:, column : column + 2 * NZ], preferred_element_type=F32
        )
        total = product[:SN] + product[SN:]
        spread[pl.ds(cell, SN, stride=PITCH), :] = total[:, :NZ]
        spread[pl.ds(cell + 1, SN, stride=PITCH), :] = total[:, NZ:]
    for snap in range(SN):
        modes[snap * CELLS : (snap + 1) * CELLS, :] = spread[
            snap * PITCH : snap * PITCH + CELLS, :
        ].astype(BF16)


def shape(*dims, dtype=F32):
    return jax.ShapeDtypeStruct(dims, dtype)


def onchip(*dims, dtype=F32):
    return pltpu.VMEM(dims, dtype)


def far(*values):
    return [pltpu.with_memory_space_constraint(v, pltpu.HBM) for v in values]


def near(*values):
    return [pltpu.with_memory_space_constraint(v, pltpu.VMEM) for v in values]


def cost(flops, bytes_accessed):
    return pl.CostEstimate(flops=flops, bytes_accessed=bytes_accessed, transcendentals=0)


def whole_gram(gram):
    plane = 2 * lax.axis_size("gy")
    planes = lax.axis_size("gx") // 2
    within = [[k * plane + m for m in range(plane)] for k in range(planes)]
    across = [[k * plane + m for k in range(planes)] for m in range(plane)]
    rows = SN // plane

    def exchange(value, groups):
        return lax.all_to_all(value, ("gx", "gy"), 0, 0, axis_index_groups=groups)

    mine = jnp.sum(exchange(gram.reshape(plane, rows, SN), within), axis=0)
    mine = jnp.sum(exchange(jnp.broadcast_to(mine[None], (planes, rows, SN)), across), axis=0)
    pieces = exchange(jnp.broadcast_to(mine[None], (plane, rows, SN)), within)
    return pieces.reshape(SN, SN)


def per_device(snapshots, viscosity, velocity):
    flat = snapshots.reshape(ROWS, NZ)
    visc = viscosity.reshape(CELLS, NZ)
    vel = velocity.reshape(3 * CELLS, NZ)
    gyd, gyu, gxd, gxu = pl.pallas_call(
        pack_kernel,
        out_shape=(
            onchip(GY_ROWS + 2 * NI, NZ),
            onchip(GY_ROWS + 2 * NI, NZ),
            onchip(GX_ROWS + 2 * NJ, NZ),
            onchip(GX_ROWS + 2 * NJ, NZ),
        ),
        in_specs=[ANY, ANY],
        out_specs=[VMEM] * 4,
        scratch_shapes=[
            pltpu.VMEM((ROWS, NZ), F32),
            pltpu.VMEM((SN * PITCH, NZ), F32),
            pltpu.VMEM((CELLS, NZ), F32),
            pltpu.SemaphoreType.DMA((5,)),
        ],
        compiler_params=pltpu.CompilerParams(vmem_limit_bytes=LIMIT),
        cost_estimate=cost(0, 6 << 20),
    )(*far(flat, visc))

    def shifted(value, axis, step):
        peers = lax.axis_size(axis)
        pairs = [(k, k + step) for k in range(peers) if 0 <= k + step < peers]
        return lax.ppermute(value, axis, pairs)

    hym, hyp = shifted(gyu, "gy", 1), shifted(gyd, "gy", -1)
    hxm, hxp = shifted(gxu, "gx", 1), shifted(gxd, "gx", -1)
    base = pl.pallas_call(
        local_kernel,
        out_shape=onchip(ROWS, NZ),
        in_specs=[VMEM] * 6,
        out_specs=VMEM,
        compiler_params=pltpu.CompilerParams(vmem_limit_bytes=LIMIT),
        cost_estimate=cost(40 * ROWS * NZ, 5 << 20),
    )(*near(gyd, gyu, hxm, hxp), visc, vel)
    count_cells = CELLS * NZ * lax.axis_size("gx") * lax.axis_size("gy")
    split_p, acc_up = pl.pallas_call(
        upper_rows_kernel,
        out_shape=(onchip(2 * SN, CELLS * NZ // 2, dtype=BF16), onchip(2 * SN, 2 * SN)),
        in_specs=[VMEM] * 6,
        out_specs=[VMEM] * 2,
        compiler_params=pltpu.CompilerParams(vmem_limit_bytes=LIMIT),
        cost_estimate=cost(4 * SN * SN * CELLS * NZ, 4 << 20),
    )(*near(base, gyd, gyu, hyp), visc, vel)
    split_m, gram = pl.pallas_call(
        functools.partial(lower_rows_kernel, 1.0 / count_cells),
        out_shape=(onchip(2 * SN, CELLS * NZ // 2, dtype=BF16), onchip(SN, SN)),
        in_specs=[VMEM] * 7,
        out_specs=[VMEM] * 2,
        scratch_shapes=[pltpu.VMEM((2 * SN, 2 * SN), F32)],
        compiler_params=pltpu.CompilerParams(vmem_limit_bytes=LIMIT),
        cost_estimate=cost(4 * SN * SN * CELLS * NZ, 4 << 20),
    )(*near(base, gyd, gyu, hym), visc, vel, *near(acc_up))
    total = whole_gram(gram)
    modes, factor = pl.pallas_call(
        solve_kernel,
        out_shape=(shape(ROWS, NZ, dtype=BF16), shape(SN, SN)),
        in_specs=[VMEM] * 3,
        out_specs=[VMEM] * 2,
        scratch_shapes=[
            pltpu.VMEM((SN, SN), F32),
            pltpu.VMEM((SN, SN), F32),
            pltpu.VMEM((2 * SN, 2 * SN), BF16),
            pltpu.VMEM((SN * PITCH, NZ), F32),
        ],
        compiler_params=pltpu.CompilerParams(vmem_limit_bytes=LIMIT),
        cost_estimate=cost(8 * SN * SN * CELLS * NZ, 4 << 20),
    )(*near(total, split_m, split_p))
    return modes.reshape(SN, NI, NJ, NZ), factor


def solution(mesh):
    placed = (P(None, "gx", "gy", None), P("gx", "gy", None), P(None, "gx", "gy", None))
    return jax.shard_map(
        per_device,
        mesh=mesh,
        in_specs=placed,
        out_specs=(P(None, "gx", "gy", None), P()),
        check_vma=False,
    )
```

```python
import functools

import jax
import jax.numpy as jnp
from jax import lax
from jax.experimental import pallas as pl
from jax.experimental.pallas import tpu as pltpu
from jax.sharding import PartitionSpec as P

F32 = jnp.float32
BF16 = jnp.bfloat16
SN, NI, NJ, NZ = 128, 8, 4, 128
CELLS = NI * NJ
ROWS = SN * CELLS
GY_ROWS = 2 * NI * SN
GX_ROWS = 2 * NJ * SN
PITCH = CELLS + 1
LIMIT = 20 << 20
VMEM = pl.BlockSpec(memory_space=pltpu.VMEM)
ANY = pl.BlockSpec(memory_space=pl.ANY)


def gy_at(j, i):
    return ((j % 2) * NI + i) * SN


def gx_at(layer, j):
    return (layer * NJ + j) * SN


def pack_kernel(u_hbm, visc_hbm, gyd, gyu, gxd, gxu, ubuf, turned, visc, sems):
    chunks = 4
    small = pltpu.make_async_copy(visc_hbm, visc, sems.at[chunks])
    rows = ROWS // chunks
    copies = [
        pltpu.make_async_copy(
            u_hbm.at[pl.ds(k * rows, rows)], ubuf.at[pl.ds(k * rows, rows)], sems.at[k]
        )
        for k in range(chunks)
    ]
    for copy in copies:
        copy.start()
    small.start()
    for k in range(chunks):
        copies[k].wait()
        for snap in range(k * SN // chunks, (k + 1) * SN // chunks):
            for part in range(0, CELLS, 8):
                turned[snap * PITCH + part : snap * PITCH + part + 8, :] = ubuf[
                    snap * CELLS + part : snap * CELLS + part + 8, :
                ]
        for first in range(k * SN // chunks, (k + 1) * SN // chunks, 8):
            for i in range(NI):
                for j in range(NJ):
                    tile = turned[pl.ds(first * PITCH + i * NJ + j, 8, stride=PITCH), :]
                    (gyd if j < 2 else gyu)[pl.ds(gy_at(j, i) + first, 8), :] = tile
                    if i < 2:
                        gxd[pl.ds(gx_at(i, j) + first, 8), :] = tile
                    if i >= 6:
                        gxu[pl.ds(gx_at(i - 6, j) + first, 8), :] = tile
    small.wait()
    for i in range(NI):
        for j in range(NJ):
            row = visc[pl.ds(i * NJ + j, 1), :]
            (gyd if j < 2 else gyu)[pl.ds(GY_ROWS + (j % 2) * NI + i, 1), :] = row
            if i < 2:
                gxd[pl.ds(GX_ROWS + i * NJ + j, 1), :] = row
            if i >= 6:
                gxu[pl.ds(GX_ROWS + (i - 6) * NJ + j, 1), :] = row


def local_kernel(gyd, gyu, hxm, hxp, visc, vel, out):
    lanes = lax.broadcasted_iota(jnp.int32, (8, NZ), 1)
    lane_row = lax.broadcasted_iota(jnp.int32, (1, NZ), 1)

    def source(i, j):
        if i < 0:
            return hxm, gx_at(i + 2, j)
        if i >= NI:
            return hxp, gx_at(i - NI, j)
        return (gyd if j < 2 else gyu), gy_at(j, i)

    def nu(i, j):
        if i < 0:
            return hxm[pl.ds(GX_ROWS + (i + 2) * NJ + j, 1), :]
        if i >= NI:
            return hxp[pl.ds(GX_ROWS + (i - NI) * NJ + j, 1), :]
        return visc[pl.ds(i * NJ + j, 1), :]

    def wide(row):
        return jnp.broadcast_to(row, (8, NZ))

    for i in range(NI):
        for j in range(NJ):
            mid = nu(i, j)
            vx, vy, vz = (vel[pl.ds(d * CELLS + i * NJ + j, 1), :] for d in range(3))
            ax8, ax1 = wide(vx * (8.0 / 12.0)), wide(vx * (1.0 / 12.0))
            az8, az1 = wide(vz * (8.0 / 12.0)), wide(vz * (1.0 / 12.0))
            ay8 = wide(vy * (8.0 / 12.0))
            xp, xm = wide(0.5 * (mid + nu(i + 1, j))), wide(0.5 * (mid + nu(i - 1, j)))
            nz_up = jnp.where(lane_row == NZ - 1, 0.0, pltpu.roll(mid, NZ - 1, 1))
            nz_dn = jnp.where(lane_row == 0, 0.0, pltpu.roll(mid, 1, 1))
            zp, zm = wide(0.5 * (mid + nz_up)), wide(0.5 * (mid + nz_dn))
            yp = wide(0.5 * (mid + nu(i, j + 1))) if j < NJ - 1 else None
            ym = wide(0.5 * (mid + nu(i, j - 1))) if j > 0 else None

            def group(g, carry, i=i, j=j):
                first = g * 8

                def load(ii, jj):
                    ref, base = source(ii, jj)
                    return ref[pl.ds(base + first, 8), :]

                u = load(i, j)
                p1, m1, p2, m2 = load(i + 1, j), load(i - 1, j), load(i + 2, j), load(i - 2, j)
                total = ax8 * (p1 - m1) - ax1 * (p2 - m2)
                total = total - (xp * (p1 - u) - xm * (u - m1))
                p1 = jnp.where(lanes == NZ - 1, 0.0, pltpu.roll(u, NZ - 1, 1))
                p2 = jnp.where(lanes >= NZ - 2, 0.0, pltpu.roll(u, NZ - 2, 1))
                m1 = jnp.where(lanes == 0, 0.0, pltpu.roll(u, 1, 1))
                m2 = jnp.where(lanes < 2, 0.0, pltpu.roll(u, 2, 1))
                total = total + (az8 * (p1 - m1) - az1 * (p2 - m2))
                total = total - (zp * (p1 - u) - zm * (u - m1))
                if j < NJ - 1:
                    p1 = load(i, j + 1)
                    total = total - yp * (p1 - u)
                if j > 0:
                    m1 = load(i, j - 1)
                    total = total + ym * (u - m1)
                if 0 < j < NJ - 1:
                    total = total + ay8 * (p1 - m1)
                out[pl.ds((i * NJ + j) * SN + first, 8), :] = total
                return carry

            for g in range(SN // 8):
                group(g, 0)


def over_cells(value):
    return lax.dot_general(value, value, (((1,), (1,)), ((), ())), preferred_element_type=F32)


def put_split(split, value, first, column):
    high = value.astype(BF16)
    low = (value - high.astype(F32)).astype(BF16)
    split[first : first + 16, column : column + NZ] = high
    split[SN + first : SN + first + 16, column : column + NZ] = low


def upper_rows_kernel(base, gyd, gyu, hyp, visc, vel, split, acc):
    def wide(row):
        return jnp.broadcast_to(row, (16, NZ))

    for i in range(NI):
        vy = [vel[pl.ds(CELLS + i * NJ + j, 1), :] for j in range(NJ)]
        a8, a1, a1_in = wide(vy[3] * (8.0 / 12.0)), wide(vy[3] * (1.0 / 12.0)), wide(vy[2] * (1.0 / 12.0))
        yp = wide(0.5 * (visc[pl.ds(i * NJ + 3, 1), :] + hyp[pl.ds(GY_ROWS + i, 1), :]))
        for first in range(0, SN, 16):

            def at(ref, j, first=first):
                return ref[pl.ds(gy_at(j, i) + first, 16), :]

            u0, u1, u2, u3 = at(gyd, 0), at(gyd, 1), at(gyu, 2), at(gyu, 3)
            p1, p2 = at(hyp, 0), at(hyp, 1)
            row = (i * NJ + 2) * SN + first
            put_split(split, base[row : row + 16, :] - a1_in * (p1 - u0), first, i * 2 * NZ)
            edge = (a8 * (p1 - u2) - a1 * (p2 - u1)) - yp * (p1 - u3)
            put_split(split, base[row + SN : row + SN + 16, :] + edge, first, (i * 2 + 1) * NZ)
        fresh = over_cells(split[:, i * 2 * NZ : (i + 1) * 2 * NZ])
        acc[...] = fresh if i == 0 else acc[...] + fresh


def lower_rows_kernel(scale, base, gyd, gyu, hym, visc, vel, acc_up, split, gram, acc):
    def wide(row):
        return jnp.broadcast_to(row, (16, NZ))

    for i in range(NI):
        vy = [vel[pl.ds(CELLS + i * NJ + j, 1), :] for j in range(NJ)]
        a8, a1, a1_in = wide(vy[0] * (8.0 / 12.0)), wide(vy[0] * (1.0 / 12.0)), wide(vy[1] * (1.0 / 12.0))
        ym = wide(0.5 * (visc[pl.ds(i * NJ, 1), :] + hym[pl.ds(GY_ROWS + NI + i, 1), :]))
        for first in range(0, SN, 16):

            def at(ref, j, first=first):
                return ref[pl.ds(gy_at(j, i) + first, 16), :]

            u0, u1, u2, u3 = at(gyd, 0), at(gyd, 1), at(gyu, 2), at(gyu, 3)
            m2, m1 = at(hym, 0), at(hym, 1)
            row = i * NJ * SN + first
            edge = (a8 * (u1 - m1) - a1 * (u2 - m2)) + ym * (u0 - m1)
            put_split(split, base[row : row + 16, :] + edge, first, i * 2 * NZ)
            put_split(
                split, base[row + SN : row + SN + 16, :] - a1_in * (u3 - m1), first, (i * 2 + 1) * NZ
            )
        fresh = over_cells(split[:, i * 2 * NZ : (i + 1) * 2 * NZ])
        acc[...] = acc_up[...] + fresh if i == 0 else acc[...] + fresh
    gram[...] = (
        (acc[:SN, :SN] + acc[SN:, SN:]) + (acc[:SN, SN:] + acc[SN:, :SN])
    ) * scale


def spread_lane(row, lane):
    return jnp.take_along_axis(row, jnp.full((8, SN), lane, jnp.int32), axis=1)


def pieces_of(value):
    high = value.astype(BF16).astype(F32)
    middle = (value - high).astype(BF16).astype(F32)
    return high, middle, (value - high) - middle


def eight_row_product(left, right):
    lh, lm, ll = pieces_of(left)
    rh, rm, rl = pieces_of(right)
    stacked_left = jnp.concatenate([lh, lh, lh, lm, lm, ll], axis=0).astype(BF16)
    stacked_right = jnp.concatenate([rh, rm, rl, rh, rm, rh], axis=0).astype(BF16)
    return lax.dot_general(
        stacked_left, stacked_right, (((0,), (0,)), ((), ())), preferred_element_type=F32
    )


def factorise(work, upper, inverse):
    lanes = lax.broadcasted_iota(jnp.int32, (8, SN), 1)
    depth = lax.broadcasted_iota(jnp.int32, (8, SN), 0)
    for base in range(0, SN, 8):
        panel = work[base : base + 8, :]
        rows = [jnp.broadcast_to(work[base + k : base + k + 1, :], (8, SN)) for k in range(8)]
        entry = {}
        for r in range(8):
            for c in range(r + 1):
                entry[r, c] = spread_lane(rows[c], base + r)
        lower, inv, root = {}, {}, {}
        for k in range(8):
            inv[k] = 1.0 / entry[k, k]
            root[k] = lax.rsqrt(entry[k, k])
            for r in range(k + 1, 8):
                lower[r, k] = entry[r, k] * inv[k]
                for c in range(k + 1, r + 1):
                    entry[r, c] = entry[r, c] - lower[r, k] * entry[c, k]
        inside = (lanes >= base) & (lanes < base + 8)
        fwd, fwd_u, back = {}, {}, {}
        for k in range(8):
            z = jnp.where(inside, jnp.where(lanes == base + k, 1.0, 0.0), rows[k])
            for m in range(k):
                z = z - lower[k, m] * fwd[m]
            fwd[k] = z
        scaled = [fwd[k] * inv[k] for k in range(8)]
        first = base + 8
        if first < SN:
            tile = work[first : first + 8, :]
            fresh = jnp.where(inside, 0.0, tile)
            columns = {}
            for k in range(8):
                column = jnp.broadcast_to(tile[:, base + k : base + k + 1], (8, SN))
                for m in range(k):
                    column = column - lower[k, m] * columns[m]
                columns[k] = column
                fresh = fresh - column * scaled[k]
            work[first : first + 8, :] = fresh
        for k in range(8):
            zu = rows[k]
            for m in range(k):
                zu = zu - lower[k, m] * fwd_u[m]
            fwd_u[k] = zu
            upper[base + k : base + k + 1, :] = jnp.where(lanes >= base + k, zu * root[k], 0.0)[:1]
            inverse[base + k : base + k + 1, :] = jnp.where(lanes <= base + k, fwd[k] * root[k], 0.0)[:1]
        if first + 8 >= SN:
            continue
        for k in reversed(range(8)):
            y = scaled[k]
            for m in range(k + 1, 8):
                y = y - lower[m, k] * back[m]
            back[k] = y
        stacked = back[0]
        for k in range(1, 8):
            stacked = jnp.where(depth == k, back[k], stacked)
        update = eight_row_product(panel, stacked)
        for top in range(first + 8, SN, 8):
            tile = jnp.where(inside, 0.0, work[top : top + 8, :])
            work[top : top + 8, :] = tile - update[top : top + 8, :]


def solve_kernel(gram, split_m, split_p, modes, upper, work, inverse, both, spread):
    work[...] = gram[...]
    factorise(work, upper, inverse)
    full = inverse[...]
    high = full.astype(BF16)
    low = (full - high.astype(F32)).astype(BF16)
    both[:SN, :SN] = high
    both[:SN, SN:] = high
    both[SN:, :SN] = low
    both[SN:, SN:] = low
    for cell in range(0, CELLS, 2):
        split = split_m if cell % NJ == 0 else split_p
        column = cell // NJ * 2 * NZ
        product = jnp.dot(
            both[...], split[:, column : column + 2 * NZ], preferred_element_type=F32
        )
        total = product[:SN] + product[SN:]
        spread[pl.ds(cell, SN, stride=PITCH), :] = total[:, :NZ]
        spread[pl.ds(cell + 1, SN, stride=PITCH), :] = total[:, NZ:]
    for snap in range(SN):
        modes[snap * CELLS : (snap + 1) * CELLS, :] = spread[
            snap * PITCH : snap * PITCH + CELLS, :
        ].astype(BF16)


def shape(*dims, dtype=F32):
    return jax.ShapeDtypeStruct(dims, dtype)


def onchip(*dims, dtype=F32):
    return pltpu.VMEM(dims, dtype)


def far(*values):
    return [pltpu.with_memory_space_constraint(v, pltpu.HBM) for v in values]


def near(*values):
    return [pltpu.with_memory_space_constraint(v, pltpu.VMEM) for v in values]


def cost(flops, bytes_accessed):
    return pl.CostEstimate(flops=flops, bytes_accessed=bytes_accessed, transcendentals=0)


def whole_gram(gram):
    plane = 2 * lax.axis_size("gy")
    planes = lax.axis_size("gx") // 2
    within = [[k * plane + m for m in range(plane)] for k in range(planes)]
    across = [[k * plane + m for k in range(planes)] for m in range(plane)]
    rows = SN // plane

    def exchange(value, groups):
        return lax.all_to_all(value, ("gx", "gy"), 0, 0, axis_index_groups=groups)

    mine = jnp.sum(exchange(gram.reshape(plane, rows, SN), within), axis=0)
    mine = jnp.sum(exchange(jnp.broadcast_to(mine[None], (planes, rows, SN)), across), axis=0)
    pieces = exchange(jnp.broadcast_to(mine[None], (plane, rows, SN)), within)
    return pieces.reshape(SN, SN)


def per_device(snapshots, viscosity, velocity):
    flat = snapshots.reshape(ROWS, NZ)
    visc = viscosity.reshape(CELLS, NZ)
    vel = velocity.reshape(3 * CELLS, NZ)
    gyd, gyu, gxd, gxu = pl.pallas_call(
        pack_kernel,
        out_shape=(
            onchip(GY_ROWS + 2 * NI, NZ),
            onchip(GY_ROWS + 2 * NI, NZ),
            onchip(GX_ROWS + 2 * NJ, NZ),
            onchip(GX_ROWS + 2 * NJ, NZ),
        ),
        in_specs=[ANY, ANY],
        out_specs=[VMEM] * 4,
        scratch_shapes=[
            pltpu.VMEM((ROWS, NZ), F32),
            pltpu.VMEM((SN * PITCH, NZ), F32),
            pltpu.VMEM((CELLS, NZ), F32),
            pltpu.SemaphoreType.DMA((5,)),
        ],
        compiler_params=pltpu.CompilerParams(vmem_limit_bytes=LIMIT),
        cost_estimate=cost(0, 6 << 20),
    )(*far(flat, visc))

    def shifted(value, axis, step):
        peers = lax.axis_size(axis)
        pairs = [(k, k + step) for k in range(peers) if 0 <= k + step < peers]
        return lax.ppermute(value, axis, pairs)

    hym, hyp = shifted(gyu, "gy", 1), shifted(gyd, "gy", -1)
    hxm, hxp = shifted(gxu, "gx", 1), shifted(gxd, "gx", -1)
    base = pl.pallas_call(
        local_kernel,
        out_shape=onchip(ROWS, NZ),
        in_specs=[VMEM] * 6,
        out_specs=VMEM,
        compiler_params=pltpu.CompilerParams(vmem_limit_bytes=LIMIT),
        cost_estimate=cost(40 * ROWS * NZ, 5 << 20),
    )(*near(gyd, gyu, hxm, hxp), visc, vel)
    count_cells = CELLS * NZ * lax.axis_size("gx") * lax.axis_size("gy")
    split_p, acc_up = pl.pallas_call(
        upper_rows_kernel,
        out_shape=(onchip(2 * SN, CELLS * NZ // 2, dtype=BF16), onchip(2 * SN, 2 * SN)),
        in_specs=[VMEM] * 6,
        out_specs=[VMEM] * 2,
        compiler_params=pltpu.CompilerParams(vmem_limit_bytes=LIMIT),
        cost_estimate=cost(4 * SN * SN * CELLS * NZ, 4 << 20),
    )(*near(base, gyd, gyu, hyp), visc, vel)
    split_m, gram = pl.pallas_call(
        functools.partial(lower_rows_kernel, 1.0 / count_cells),
        out_shape=(onchip(2 * SN, CELLS * NZ // 2, dtype=BF16), onchip(SN, SN)),
        in_specs=[VMEM] * 7,
        out_specs=[VMEM] * 2,
        scratch_shapes=[pltpu.VMEM((2 * SN, 2 * SN), F32)],
        compiler_params=pltpu.CompilerParams(vmem_limit_bytes=LIMIT),
        cost_estimate=cost(4 * SN * SN * CELLS * NZ, 4 << 20),
    )(*near(base, gyd, gyu, hym), visc, vel, *near(acc_up))
    total = whole_gram(gram)
    modes, factor = pl.pallas_call(
        solve_kernel,
        out_shape=(shape(ROWS, NZ, dtype=BF16), shape(SN, SN)),
        in_specs=[VMEM] * 3,
        out_specs=[VMEM] * 2,
        scratch_shapes=[
            pltpu.VMEM((SN, SN), F32),
            pltpu.VMEM((SN, SN), F32),
            pltpu.VMEM((2 * SN, 2 * SN), BF16),
            pltpu.VMEM((SN * PITCH, NZ), F32),
        ],
        compiler_params=pltpu.CompilerParams(vmem_limit_bytes=LIMIT),
        cost_estimate=cost(8 * SN * SN * CELLS * NZ, 4 << 20),
    )(*near(total, split_m, split_p))
    return modes.reshape(SN, NI, NJ, NZ), factor


def solution(mesh):
    placed = (P(None, "gx", "gy", None), P("gx", "gy", None), P(None, "gx", "gy", None))
    return jax.shard_map(
        per_device,
        mesh=mesh,
        in_specs=placed,
        out_specs=(P(None, "gx", "gy", None), P()),
        check_vma=False,
    )
```
